32 devices in a mesh: row: 8 (over z, x), col: 4 (over y, core).
Axes of the slice: x: 2, y: 2, z: 4, core: 2. Of those that a mesh axis runs over, the one named last changes fastest.
Arguments:
- feat: bfloat16 [256, 128, 256], P('row', 'col'), may hold values from -6 to 6
- noise_fine: float32 [256, 128, 256], P('row', 'col'), may hold values from -0.5 to 0.5
- noise_coarse: float32 [128, 64, 256], P('row', 'col'), may hold values from -0.5 to 0.5
- w_post: bfloat16 [2304, 256], replicated, may hold values from -0.125 to 0.125
- w_coarse: bfloat16 [2304, 256], replicated, may hold values from -0.125 to 0.125
- w_prior: bfloat16 [2304, 512], replicated, may hold values from -0.125 to 0.125
Outputs:
- grad_feat: bfloat16 [256, 128, 256], P('row', 'col')
- grad_post: float32 [589824], P(('row', 'col'))
- grad_coarse: float32 [589824], P(('row', 'col'))
- grad_prior: float32 [1179648], P(('row', 'col'))
The draws below stay inside these ranges and needn't reach their ends.
All inputs are finite; a program needn't handle non-finite values.
Results may differ from the reference program's by a relative error of at most 0.0075.
Values may be sent and summed in bfloat16 or wider, within the bound.
A program may use at most 128 MiB of HBM per device.

```python
import math
import jax
import jax.numpy as jnp

C = 256
H = 256
W = 128
H2 = 128
W2 = 64


def with_spikes(entries, own_key, source, target, parts, factor):
    def block_of(position):
        return (jnp.arange(entries.shape[position]) // (entries.shape[position] // parts)).reshape((-1,) + (1,) * (entries.ndim - 1 - position))

    first = jax.random.permutation(own_key, parts)[block_of(target)]
    far = (block_of(target) + parts // 2) % parts
    return jnp.where((block_of(source) == first) | (block_of(source) == far), factor * entries, entries)


def steps_of(rng, shape, shards, smallest, largest):
    level = 1.0
    for position, shards_of in shards:
        heights = jax.random.uniform(jax.random.fold_in(jax.random.fold_in(rng, 6), position), (shards_of,), jnp.float32, smallest / len(shards), largest / len(shards))
        level = level * jnp.repeat(jnp.exp(heights), shape[position] // shards_of).reshape((-1,) + (1,) * (len(shape) - 1 - position))
    return level


def centred(rng, dims, width, bound, cuts=(), held_as=jnp.bfloat16):
    loudness = steps_of(rng, dims, cuts, -0.22, 0.18) if cuts else 1.0
    drawn = jax.random.normal(rng, dims, jnp.float32) * width * loudness
    return jnp.minimum(jnp.maximum(drawn, -bound), bound).astype(held_as)


def bell_draw_with(stream_key, shape, scale, limit, pieces, heavy, held_as=jnp.bfloat16):
    entries = scale * jax.random.normal(stream_key, shape, jnp.float32)
    if pieces:
        entries = entries * steps_of(stream_key, shape, pieces, -0.22, 0.18)
    return jnp.clip(with_spikes(entries, jax.random.fold_in(stream_key, 3), *heavy), -limit, limit).astype(held_as)


def setup_inputs(seed: int = 0) -> dict:
    streams_of = jax.random.split(jax.random.key(seed), 7)
    return {
        "feat": bell_draw_with(streams_of[0], (H, W, C), 1.0, 6.0, ((0, 8), (1, 4)), (0, 2, 8, 2.0)),
        "noise_fine": jnp.clip(jax.random.uniform(streams_of[1], (H, W, C), jnp.float32, -0.5, 0.5) * steps_of(streams_of[1], (H, W, C), ((0, 8), (1, 4)), -0.4, 0.0), -0.5, 0.5),
        "noise_coarse": jnp.clip(jax.random.uniform(streams_of[2], (H2, W2, C), jnp.float32, -0.5, 0.5) * steps_of(streams_of[2], (H2, W2, C), ((0, 8), (1, 4)), -0.4, 0.0), -0.5, 0.5),
        "w_post": centred(streams_of[3], (9 * C, C), (9 * C) ** -0.5, 0.125),
        "w_coarse": centred(streams_of[4], (9 * C, C), (9 * C) ** -0.5, 0.125),
        "w_prior": centred(streams_of[5], (9 * C, 2 * C), (9 * C) ** -0.5, 0.125),
    }


def conv_taps(field, weight):
    size_r, size_c, chans = field.shape
    padded = jnp.pad(field, ((1, 1), (1, 1), (0, 0)))
    total = jnp.zeros((size_r * size_c, weight.shape[1]), jnp.float32)
    for tap_row in range(3):
        for tap_col in range(3):
            index = 3 * tap_row + tap_col
            piece = padded[tap_row:tap_row + size_r, tap_col:tap_col + size_c].reshape(-1, chans)
            total = total + jnp.dot(piece, weight[index * chans:(index + 1) * chans], preferred_element_type=jnp.float32)
    return total.reshape(size_r, size_c, weight.shape[1])

def conv_back(grad, weight):
    size_r, size_c, chans_g = grad.shape
    chans_in = weight.shape[0] // 9
    padded = jnp.pad(grad, ((1, 1), (1, 1), (0, 0)))
    total = jnp.zeros((size_r * size_c, chans_in), jnp.float32)
    for tap_row in range(3):
        for tap_col in range(3):
            index = 3 * tap_row + tap_col
            piece = padded[2 - tap_row:2 - tap_row + size_r, 2 - tap_col:2 - tap_col + size_c].reshape(-1, chans_g)
            total = total + jnp.dot(piece, weight[index * chans_in:(index + 1) * chans_in].T, preferred_element_type=jnp.float32)
    return total.reshape(size_r, size_c, chans_in)

def weight_grad(field, grad):
    size_r, size_c, chans = field.shape
    padded = jnp.pad(field, ((1, 1), (1, 1), (0, 0)))
    flat_grad = grad.reshape(-1, grad.shape[-1])
    blocks = []
    for tap_row in range(3):
        for tap_col in range(3):
            piece = padded[tap_row:tap_row + size_r, tap_col:tap_col + size_c].reshape(-1, chans)
            blocks.append(jnp.dot(piece.T, flat_grad, preferred_element_type=jnp.float32))
    return jnp.concatenate(blocks, axis=0)

def repeat_two(field):
    return jnp.repeat(jnp.repeat(field, 2, axis=0), 2, axis=1)

def reference(feat, noise_fine, noise_coarse, w_post, w_coarse, w_prior):
    full_r, full_c, chans = feat.shape
    grad_scale = 1.0 / math.sqrt(full_r * full_c)
    fine = conv_taps(feat, w_post) + noise_fine
    pooled = fine.reshape(full_r // 2, 2, full_c // 2, 2, chans).mean(axis=(1, 3)).astype(jnp.bfloat16)
    coarse = conv_taps(pooled, w_coarse) + noise_coarse
    context = repeat_two(coarse.astype(jnp.bfloat16))
    prior = conv_taps(context, w_prior)
    prior_mean = prior[..., :chans]
    raw_scale = prior[..., chans:]
    prior_scale = jax.nn.softplus(raw_scale) + 0.5
    deviation = fine - prior_mean
    residual_term = deviation / (prior_scale * prior_scale)
    scale_term = 1.0 / prior_scale - deviation * deviation / (prior_scale * prior_scale * prior_scale)
    dprior = jnp.concatenate([-residual_term, scale_term * jax.nn.sigmoid(raw_scale)], axis=-1).astype(jnp.bfloat16)
    grad_prior = weight_grad(context, dprior) * grad_scale
    back_context = conv_back(dprior, w_prior)
    gcoarse = (coarse + back_context.reshape(full_r // 2, 2, full_c // 2, 2, chans).sum(axis=(1, 3))).astype(jnp.bfloat16)
    grad_coarse = weight_grad(pooled, gcoarse) * grad_scale
    back_pooled = conv_back(gcoarse, w_coarse)
    gfine = (residual_term + 0.25 * repeat_two(back_pooled)).astype(jnp.bfloat16)
    grad_post = weight_grad(feat, gfine) * grad_scale
    grad_feat = conv_back(gfine, w_post).astype(jnp.bfloat16)
    return (grad_feat, grad_post.reshape(-1), grad_coarse.reshape(-1), grad_prior.reshape(-1))
```

```python
import functools
import math

import jax
import jax.numpy as jnp
from jax import lax
from jax.experimental import pallas as pl
from jax.experimental.pallas import tpu as pltpu
from jax.sharding import PartitionSpec as P

F32 = jnp.float32
BF16 = jnp.bfloat16
EDGE = 8


LANES = 128


def put(ref, at, values):
    for d in range(values.shape[1] // LANES):
        ref[d, at, :] = values[:, d * LANES : (d + 1) * LANES]


def get(ref, at):
    return jnp.concatenate([ref[d, at, :] for d in range(ref.shape[0])], axis=1)


DIRECTIONS = ((-1, 0), (1, 0), (0, -1), (0, 1), (-1, -1), (-1, 1), (1, -1), (1, 1))
OPPOSITE = (1, 0, 3, 2, 7, 6, 5, 4)
UP, DOWN, LEFT, RIGHT, UP_LEFT, UP_RIGHT, DOWN_LEFT, DOWN_RIGHT = range(8)
TAPS = (((0,), (1, 2)), ((0, 1), (2,)))


def round_up(n, m):
    return -(-n // m) * m


def tile_kernel(
    dims,
    feat,
    noise_fine,
    noise_coarse,
    w_post,
    w_coarse,
    w_prior,
    grad_feat,
    out_post,
    out_coarse,
    out_prior,
    fine,
    err,
    coarse,
    s_fine,
    s_pool,
    s_noise,
    s_ctx,
    s_pair,
    x_feat,
    x_pool,
    side_pool,
    x_ctx,
    side_ctx,
    w_sums,
    g_main,
    g_side,
    boxes,
    own_gfi,
    edges,
    halos,
    sums,
    outgoing,
    incoming,
    sems,
    chain_sems,
):
    x_gco, x_gfi = x_ctx, x_feat
    rows, cols, chans, scale, n_row, n_col = dims
    mix = s_pair.at[0, pl.ds(0, chans // LANES)]
    h, w = rows // 2, cols // 2
    cells = h * w
    r = lax.axis_index("row")
    c = lax.axis_index("col")
    has_up, has_down = r > 0, r < n_row - 1
    has_left, has_right = c > 0, c < n_col - 1
    vertical = {-1: has_up, 0: None, 1: has_down}
    horizontal = {-1: has_left, 0: None, 1: has_right}

    def neighbour(d):
        down, right = DIRECTIONS[d]
        device = {}
        if down:
            device["row"] = r + down
        if right:
            device["col"] = c + right
        if not right:
            return vertical[down], device
        if not down:
            return horizontal[right], device
        return jnp.logical_and(vertical[down], horizontal[right]), device

    sides = [neighbour(d) for d in range(8)]

    halos[...] = jnp.zeros_like(halos)
    barrier = pltpu.get_barrier_semaphore()
    for has, device in sides:
        @pl.when(has)
        def _(device=device):
            pl.semaphore_signal(
                barrier, inc=1, device_id=device, device_id_type=pl.DeviceIdType.MESH
            )
    count = n_row * n_col
    bits = count.bit_length() - 1
    col_bits = n_col.bit_length() - 1
    me = r * n_col + c

    def bit_of(b):
        return me // 2**b % 2

    def partner(b):
        if b < col_bits:
            return {"col": c + 2**b * (1 - 2 * bit_of(b))}
        return {"row": r + 2 ** (b - col_bits) * (1 - 2 * bit_of(b))}

    for b in range(bits):
        pl.semaphore_signal(
            barrier, inc=1, device_id=partner(b), device_id_type=pl.DeviceIdType.MESH
        )

    for ref in (s_fine, s_pool, s_noise, s_ctx, fine):
        ref[...] = jnp.zeros_like(ref)

    def enter():
        pl.semaphore_wait(barrier, bits + sum(has.astype(jnp.int32) for has, _device in sides))

    def each(n, body):
        if n <= 16:
            for j in range(n):
                body(j)
        else:
            pl.loop(0, n)(body)

    def chain(number, order, out, out_at):
        acc, send, recv = sums[number], outgoing[number], incoming[number]
        state = {"step": 0, "copy": None}

        def offset(k):
            return count - (count >> k)

        def step():
            k = state["step"]
            if k > bits:
                return
            state["step"] = k + 1
            if k > 0:
                state["copy"].wait()
            if k == bits:
                total = acc[me] + recv[offset(k - 1)].astype(F32)
                per = total.shape[0]
                stride = out.shape[0] // per
                for d in range(total.shape[1] // LANES):
                    out[pl.ds(out_at // LANES + d, per, stride=stride), :] = total[
                        :, d * LANES : (d + 1) * LANES
                    ]
                return
            bit = order[k]
            free = [b for b in range(bits) if b not in order[:k]]
            rest = [b for b in free if b != bit]
            place = free.index(bit)
            fixed = sum((bit_of(b) * 2**b for b in order[:k]), 0)
            n = count >> (k + 1)

            def value(j, choice):
                index = fixed + choice * 2**bit
                for q, b in enumerate(rest):
                    index = index + j // 2**q % 2 * 2**b
                total = acc[index]
                if k > 0:
                    slot = j // 2**place * 2 ** (place + 1) + choice * 2**place + j % 2**place
                    total = total + recv[offset(k - 1) + slot].astype(F32)
                return index, total

            def fill(j):
                send[j] = value(j, 1 - bit_of(bit))[1].astype(BF16)

            each(n, fill)
            state["copy"] = pltpu.make_async_remote_copy(
                src_ref=send.at[pl.ds(0, n)],
                dst_ref=recv.at[pl.ds(offset(k), n)],
                send_sem=chain_sems.at[number, k, 0],
                recv_sem=chain_sems.at[number, k, 1],
                device_id=partner(bit),
                device_id_type=pl.DeviceIdType.MESH,
            )
            state["copy"].start()

            def keep(j):
                index, total = value(j, bit_of(bit))
                acc[index] = total

            if k > 0:
                each(n, keep)

        return step


    near, rest = [0], list(range(1, bits))
    first = near + rest
    second = near + rest[1::-1] + rest[2:]
    third = near + rest[2:3] + rest[:2] + rest[3:]
    half = chans // 2
    post_1 = chain(0, first, out_post, 0)
    post_2 = chain(1, second, out_post, half)
    middle = chain(2, third, out_coarse, 0)
    prior_1 = chain(3, first, out_prior, 0)
    prior_2 = chain(4, second, out_prior, chans)
    parts_post = ((sums[0], 0), (sums[1], half))
    parts_coarse = ((sums[2], 0),)
    parts_prior = ((sums[3], 0), (sums[4], chans))

    def spread(parts, start, values):
        height = values.shape[0]
        for acc, at in parts:
            per, width = acc.shape[1:]
            row = start
            while row < start + height:
                inner = row % per
                size = min(per - inner, start + height - row)
                acc[row // per, inner : inner + size] = values[
                    row - start : row - start + size, at : at + width
                ]
                row += size


    def copies(index, sizes):
        found = []
        for d in range(8):
            size = sizes[0] if d < 4 else sizes[1]
            found.append(
                pltpu.make_async_remote_copy(
                    src_ref=edges.at[index, d, pl.ds(0, size)],
                    dst_ref=halos.at[index, OPPOSITE[d], pl.ds(0, size)],
                    send_sem=sems.at[index, d],
                    recv_sem=sems.at[index, 8 + OPPOSITE[d]],
                    device_id=sides[d][1],
                    device_id_type=pl.DeviceIdType.MESH,
                )
            )
        return found

    def start(index, sizes, parts):
        found = copies(index, sizes)
        for d in (4, 5, 6, 7, 0, 1, 2, 3):
            at = 0
            for part in parts[d]:
                edges[index, d, at : at + part.shape[0], :] = part.astype(BF16)
                at += part.shape[0]
            pl.when(sides[d][0])(found[d].start)
        return found

    def finish(found):
        for d in range(8):
            @pl.when(sides[d][0])
            def _(d=d):
                found[d].wait_send()
                found[OPPOSITE[d]].wait_recv()

    def halo(index, d, at, size):
        return halos[index, d, at : at + size, :].astype(F32)

    def view(x, t, u):
        return x[t % 2, u + 1, pl.ds(w if t >= 1 else 0, cells), :]

    def dot_in(x, g):
        return lax.dot_general(x, g, (((0,), (0,)), ((), ())), preferred_element_type=F32)

    def dot_out(g, weights):
        return lax.dot_general(g, weights, (((1,), (1,)), ((), ())), preferred_element_type=F32)

    def tap_of(weights, a, b):
        k = weights.shape[0] // 9
        return weights[(3 * a + b) * k : (3 * a + b + 1) * k, :]

    fine_stride = cols + 2 * EDGE
    stride = w + 2 * EDGE
    extra = round_up(h + 1, 16)
    side = round_up(h + 2, 8)
    phases = [(p, q) for p in range(2) for q in range(2)]

    for i in range(rows):
        put(
            s_fine,
            pl.ds((i + 1) * fine_stride + EDGE, cols),
            feat[pl.ds(i * cols, cols), :].astype(F32),
        )
    for i in range(h):
        put(s_noise, pl.ds((i + 1) * stride + EDGE, w), noise_coarse[pl.ds(i * w, w), :])
    top, bottom = feat[0:cols, :], feat[(rows - 1) * cols :, :]
    noise_top, noise_bottom = noise_coarse[0:w, :], noise_coarse[(h - 1) * w :, :]
    parts = [
        (top, noise_top),
        (bottom, noise_bottom),
        (
            get(s_fine, pl.ds(fine_stride + EDGE, rows, stride=fine_stride)),
            get(s_noise, pl.ds(stride + EDGE, h, stride=stride)),
        ),
        (
            get(s_fine, pl.ds(fine_stride + EDGE + cols - 1, rows, stride=fine_stride)),
            get(s_noise, pl.ds(stride + EDGE + w - 1, h, stride=stride)),
        ),
        (top[0:w], noise_top),
        (top[cols - w :], noise_top),
        (bottom[0:w], noise_bottom),
        (bottom[cols - w :], noise_bottom),
    ]
    enter()
    found = start(0, (cols + w, 2 * w), parts)

    for p, q in phases:
        for kr in range(2):
            for kc in range(2):
                total = None
                for a in TAPS[p][kr]:
                    for b in TAPS[q][kc]:
                        part = tap_of(w_prior, a, b).astype(F32)
                        total = part if total is None else total + part
                w_sums[((2 * p + kr) * 2 + q) * 2 + kc] = total.astype(BF16)

    def own(p):
        return slice(p * w, p * w + cells)

    put(mix, pl.ds(0, rows * cols), noise_fine[...])
    for p, q in phases:
        for i in range(h):
            fine[2 * p + q, (i + p) * w : (i + p + 1) * w, :] = get(
                mix, pl.ds((2 * i + p) * cols + q, w, stride=2)
            )

    def fill_feat(i, ms):
        p = i % 2
        at = (i - p) // 2 + p
        for m in ms:
            x_feat[p, m, at * w : (at + 1) * w, :] = get(
                s_fine, pl.ds((i + 1) * fine_stride + EDGE - 1 + m, w, stride=2)
            ).astype(BF16)

    for i in range(rows):
        fill_feat(i, (1, 2))
    finish(found)
    put(s_fine, pl.ds(EDGE, cols), halo(0, UP, 0, cols))
    put(s_fine, pl.ds((rows + 1) * fine_stride + EDGE, cols), halo(0, DOWN, 0, cols))
    put(s_fine, pl.ds(fine_stride + EDGE - 1, rows, stride=fine_stride), halo(0, LEFT, 0, rows))
    put(s_fine, pl.ds(fine_stride + EDGE + cols, rows, stride=fine_stride), halo(0, RIGHT, 0, rows))
    put(s_fine, pl.ds(EDGE - 1, 1), halo(0, UP_LEFT, 0, w)[w - 1 :])
    put(s_fine, pl.ds(EDGE + cols, 1), halo(0, UP_RIGHT, 0, w)[0:1])
    last = (rows + 1) * fine_stride + EDGE
    put(s_fine, pl.ds(last - 1, 1), halo(0, DOWN_LEFT, 0, w)[w - 1 :])
    put(s_fine, pl.ds(last + cols, 1), halo(0, DOWN_RIGHT, 0, w)[0:1])
    for i in range(rows):
        fill_feat(i, (0, 3))
    fill_feat(-1, (0, 1, 2, 3))
    fill_feat(rows, (0, 1, 2, 3))

    pooled = None
    for p, q in phases:
        total = None
        for a in range(3):
            for b in range(3):
                part = jnp.dot(
                    view(x_feat, p + a - 1, q + b - 1),
                    tap_of(w_post, a, b),
                    preferred_element_type=F32,
                )
                total = part if total is None else total + part
        total = total + fine[2 * p + q, own(p), :]
        fine[2 * p + q, own(p), :] = total
        pooled = total if pooled is None else pooled + total
    pooled = (0.25 * pooled).astype(BF16).astype(F32)
    for i in range(h):
        put(s_pool, pl.ds((i + 2) * stride + EDGE, w), pooled[i * w : (i + 1) * w])

    def line(p, q, i):
        return fine[2 * p + q, (i + p) * w : (i + p + 1) * w, :]

    def column(values, j):
        put(mix, pl.ds(0, cells), values)
        return get(mix, pl.ds(j, h, stride=w))

    pool_top, pool_bottom = pooled[0 : 2 * w], pooled[(h - 2) * w :]

    def pool_column(j):
        return get(s_pool, pl.ds(2 * stride + EDGE + j, h, stride=stride))

    lefts = [column(fine[2 * p, own(p), :], 0) for p in range(2)]
    rights = [column(fine[2 * p + 1, own(p), :], w - 1) for p in range(2)]
    parts = [
        (pool_top, line(0, 0, 0), line(0, 1, 0)),
        (pool_bottom, line(1, 0, h - 1), line(1, 1, h - 1)),
        (pool_column(0), pool_column(1), *lefts),
        (pool_column(w - 2), pool_column(w - 1), *rights),
        (pool_top, line(0, 0, 0)),
        (pool_top, line(0, 1, 0)),
        (pool_bottom, line(1, 0, h - 1)),
        (pool_bottom, line(1, 1, h - 1)),
    ]
    found = start(1, (4 * w, 3 * w), parts)
    for i in range(h):
        put(s_noise, pl.ds((i + 1) * stride + EDGE, w), noise_coarse[pl.ds(i * w, w), :])
    put(s_noise, pl.ds(EDGE, w), halo(0, UP, cols, w))
    put(s_noise, pl.ds((h + 1) * stride + EDGE, w), halo(0, DOWN, cols, w))
    put(s_noise, pl.ds(stride + EDGE - 1, h, stride=stride), halo(0, LEFT, rows, h))
    put(s_noise, pl.ds(stride + EDGE + w, h, stride=stride), halo(0, RIGHT, rows, h))
    put(s_noise, pl.ds(EDGE - 1, 1), halo(0, UP_LEFT, w, w)[w - 1 :])
    put(s_noise, pl.ds(EDGE + w, 1), halo(0, UP_RIGHT, w, w)[0:1])
    last = (h + 1) * stride + EDGE
    put(s_noise, pl.ds(last - 1, 1), halo(0, DOWN_LEFT, w, w)[w - 1 :])
    put(s_noise, pl.ds(last + w, 1), halo(0, DOWN_RIGHT, w, w)[0:1])
    finish(found)
    for k in range(2):
        put(s_pool, pl.ds(k * stride + EDGE, w), halo(1, UP, k * w, w))
        put(s_pool, pl.ds((h + 2 + k) * stride + EDGE, w), halo(1, DOWN, k * w, w))
        put(s_pool, pl.ds(2 * stride + EDGE - 2 + k, h, stride=stride), halo(1, LEFT, k * h, h))
        put(s_pool, pl.ds(2 * stride + EDGE + w + k, h, stride=stride), halo(1, RIGHT, k * h, h))
        put(s_pool, pl.ds(k * stride + EDGE - 2, 2), halo(1, UP_LEFT, k * w, w)[w - 2 :])
        put(s_pool, pl.ds(k * stride + EDGE + w, 2), halo(1, UP_RIGHT, k * w, w)[0:2])
        at = (h + 2 + k) * stride + EDGE
        put(s_pool, pl.ds(at - 2, 2), halo(1, DOWN_LEFT, k * w, w)[w - 2 :])
        put(s_pool, pl.ds(at + w, 2), halo(1, DOWN_RIGHT, k * w, w)[0:2])
    base = cells + w
    for q in range(2):
        fine[q, cells : cells + w, :] = halo(1, DOWN, (2 + q) * w, w)
        fine[2 + q, 0:w, :] = halo(1, UP, (2 + q) * w, w)
    for p in range(2):
        fine[2 * p, base + p : base + p + h, :] = halo(1, RIGHT, (2 + p) * h, h)
        fine[2 * p + 1, base + p : base + p + h, :] = halo(1, LEFT, (2 + p) * h, h)
    fine[3, base : base + 1, :] = halo(1, UP_LEFT, 2 * w, w)[w - 1 :]
    fine[2, base : base + 1, :] = halo(1, UP_RIGHT, 2 * w, w)[0:1]
    fine[1, base + h : base + h + 1, :] = halo(1, DOWN_LEFT, 2 * w, w)[w - 1 :]
    fine[0, base + h : base + h + 1, :] = halo(1, DOWN_RIGHT, 2 * w, w)[0:1]

    for i in range(h + 4):
        for b in range(3):
            x_pool[b, i * w : (i + 1) * w, :] = get(
                s_pool, pl.ds(i * stride + EDGE + b - 1, w)
            ).astype(BF16)
    for a in range(3):
        for b in range(3):
            both = [
                get(s_pool, pl.ds(a * stride + EDGE - 2 + b, side, stride=stride)),
                get(s_pool, pl.ds(a * stride + EDGE + w - 1 + b, side, stride=stride)),
            ]
            side_pool[3 * a + b] = jnp.concatenate(both, axis=0).astype(BF16)
    ring = (h + 2) * w
    noise = jnp.concatenate(
        [get(s_noise, pl.ds(i * stride + EDGE, w)) for i in range(h + 2)]
        + [
            get(s_noise, pl.ds(EDGE - 1, side, stride=stride)),
            get(s_noise, pl.ds(EDGE + w, side, stride=stride)),
        ],
        axis=0,
    )
    total = None
    for a in range(3):
        for b in range(3):
            x = jnp.concatenate([x_pool[b, pl.ds(a * w, ring), :], side_pool[3 * a + b]], axis=0)
            part = jnp.dot(x, tap_of(w_coarse, a, b), preferred_element_type=F32)
            total = part if total is None else total + part
    total = total + noise
    coarse[...] = total[w : w + cells]
    total = total.astype(BF16).astype(F32)
    put(s_ctx, pl.ds(EDGE, w), jnp.where(has_up, total[0:w], 0.0))
    for i in range(1, h + 1):
        put(s_ctx, pl.ds(i * stride + EDGE, w), total[i * w : (i + 1) * w])
    put(s_ctx, pl.ds((h + 1) * stride + EDGE, w), jnp.where(has_down, total[ring - w : ring], 0.0))
    place = lax.broadcasted_iota(jnp.int32, (side, chans), 0)
    first = jnp.where(has_up, 0, 1)
    limit = jnp.where(has_down, h + 2, h + 1)
    inside = jnp.logical_and(place >= first, place < limit)
    for at, has, values in (
        (EDGE - 1, has_left, total[ring : ring + side]),
        (EDGE + w, has_right, total[ring + side :]),
    ):
        put(
            s_ctx,
            pl.ds(at, side, stride=stride),
            jnp.where(jnp.logical_and(inside, has), values, 0.0),
        )
    for i in range(h + 2):
        for k in range(3):
            x_ctx[k, i * w : (i + 1) * w, :] = get(
                s_ctx, pl.ds(i * stride + EDGE + k - 1, w)
            ).astype(BF16)
    for q in range(2):
        for kr in range(2):
            for kc in range(2):
                at = kr * stride + EDGE + (w - 1 if q == 0 else -1) + kc
                side_ctx[(2 * q + kr) * 2 + kc] = get(
                    s_ctx, pl.ds(at, extra, stride=stride)
                ).astype(BF16)

    place = lax.broadcasted_iota(jnp.int32, (extra, 2 * chans), 0)
    for p, q in phases:
        prior = None
        for kr in range(2):
            for kc in range(2):
                x = jnp.concatenate(
                    [x_ctx[q + kc, pl.ds(kr * w, base), :], side_ctx[(2 * q + kr) * 2 + kc]],
                    axis=0,
                )
                part = jnp.dot(
                    x, w_sums[((2 * p + kr) * 2 + q) * 2 + kc], preferred_element_type=F32
                )
                prior = part if prior is None else prior + part
        raw = prior[:, chans:]
        small = jnp.exp(-jnp.abs(raw))
        sigma = jnp.maximum(raw, 0.0) + jnp.log1p(small) + 0.5
        gate = jnp.where(raw >= 0, 1.0, small) / (1.0 + small)
        inverse = 1.0 / sigma
        ratio = (fine[2 * p + q] - prior[:, :chans]) * inverse
        residual = ratio * inverse
        err[2 * p + q] = residual[own(p)]
        slope = (inverse - ratio * ratio * inverse) * gate
        both = jnp.concatenate([-residual, slope], axis=1).astype(BF16).astype(F32)
        if p == 0:
            g_main[q, 0:cells, :] = both[0:cells]
            g_main[q, cells:, :] = jnp.where(has_down, both[cells:base], 0.0)
            inside = jnp.logical_or(has_down, place < h)
        else:
            g_main[2 + q, 0:w, :] = jnp.where(has_up, both[0:w], 0.0)
            g_main[2 + q, w:, :] = both[w:base]
            inside = jnp.logical_or(has_up, place > 0)
        inside = jnp.logical_and(inside, has_left if q else has_right)
        g_side[2 * p + q] = jnp.where(inside, both[base:], 0.0)

    windows = ((1, 1), (0, 1), (0, 0))
    for a in range(3):
        i0, i1 = windows[a]
        for q in range(2):
            total = g_main[q, pl.ds(i0 * w, cells), :] + g_main[2 + q, pl.ds(i1 * w, cells), :]
            for i in range(h):
                put(s_pair.at[q], pl.ds(i * stride + EDGE, w), total[i * w : (i + 1) * w])
            total = g_side[q, i0 : i0 + h, :] + g_side[2 + q, i1 : i1 + h, :]
            put(s_pair.at[q], pl.ds(EDGE - 1 if q else EDGE + w, h, stride=stride), total)
        for i in range(h):
            at = i * stride + EDGE
            even, odd = get(s_pair.at[0], pl.ds(at, w)), get(s_pair.at[1], pl.ds(at, w))
            here = slice(i * w, (i + 1) * w)
            boxes[3 * a, here, :] = (odd + get(s_pair.at[0], pl.ds(at + 1, w))).astype(BF16)
            boxes[3 * a + 1, here, :] = (even + odd).astype(BF16)
            boxes[3 * a + 2, here, :] = (get(s_pair.at[1], pl.ds(at - 1, w)) + even).astype(BF16)

    for tap in range(9):
        spread(
            parts_prior,
            tap * chans,
            scale * dot_in(x_ctx[1, pl.ds(w, cells), :], boxes[tap]),
        )
    prior_1()
    prior_2()
    total = None
    for tap in range(9):
        part = dot_out(boxes[tap], tap_of(w_prior, tap // 3, tap % 3))
        total = part if total is None else total + part
    total = (coarse[...] + total).astype(BF16).astype(F32)

    def pad_lines(values):
        for i in range(h):
            put(s_pool, pl.ds((i + 1) * stride + EDGE, w), values[i * w : (i + 1) * w])

    pad_lines(total)
    parts = [
        (total[0:w],),
        (total[cells - w :],),
        (get(s_pool, pl.ds(stride + EDGE, h, stride=stride)),),
        (get(s_pool, pl.ds(stride + EDGE + w - 1, h, stride=stride)),),
        (total[0:w],),
        (total[0:w],),
        (total[cells - w :],),
        (total[cells - w :],),
    ]
    found = start(2, (w, w), parts)
    gco = total.astype(BF16)
    for a in range(3):
        for b in range(3):
            spread(
                parts_coarse,
                (3 * a + b) * chans,
                scale * dot_in(x_pool[b, pl.ds((a + 1) * w, cells), :], gco),
            )
    middle()
    prior_1()
    prior_2()
    finish(found)

    put(s_pool, pl.ds(EDGE, w), halo(2, UP, 0, w))
    put(s_pool, pl.ds((h + 1) * stride + EDGE, w), halo(2, DOWN, 0, w))
    put(s_pool, pl.ds(stride + EDGE - 1, h, stride=stride), halo(2, LEFT, 0, h))
    put(s_pool, pl.ds(stride + EDGE + w, h, stride=stride), halo(2, RIGHT, 0, h))
    put(s_pool, pl.ds(EDGE - 1, 1), halo(2, UP_LEFT, 0, w)[w - 1 :])
    put(s_pool, pl.ds(EDGE + w, 1), halo(2, UP_RIGHT, 0, w)[0:1])
    last = (h + 1) * stride + EDGE
    put(s_pool, pl.ds(last - 1, 1), halo(2, DOWN_LEFT, 0, w)[w - 1 :])
    put(s_pool, pl.ds(last + w, 1), halo(2, DOWN_RIGHT, 0, w)[0:1])
    for i in range(h + 2):
        for k in range(3):
            x_gco[k, i * w : (i + 1) * w, :] = get(
                s_pool, pl.ds(i * stride + EDGE + k - 1, w)
            ).astype(BF16)
    total = None
    for a in range(3):
        for b in range(3):
            part = dot_out(x_gco[2 - b, pl.ds((2 - a) * w, cells), :], tap_of(w_coarse, a, b))
            total = part if total is None else total + part
    total = 0.25 * total

    for p, q in phases:
        own_gfi[2 * p + q] = (err[2 * p + q] + total).astype(BF16)

    def s_gfi(q):
        return s_pair.at[q, pl.ds(0, chans // LANES)]

    def gfi_line(p, q, i):
        return own_gfi[2 * p + q, i * w : (i + 1) * w, :]

    for p, q in phases:
        for i in range(h):
            put(
                s_gfi(q),
                pl.ds((i + p * h) * stride + EDGE, w),
                own_gfi[2 * p + q, i * w : (i + 1) * w, :].astype(F32),
            )

    def gfi_column(p, q):
        at = p * h * stride + EDGE + (w - 1 if q else 0)
        return get(s_gfi(q), pl.ds(at, h, stride=stride))

    parts = [
        (gfi_line(0, 0, 0), gfi_line(0, 1, 0)),
        (gfi_line(1, 0, h - 1), gfi_line(1, 1, h - 1)),
        (gfi_column(0, 0), gfi_column(1, 0)),
        (gfi_column(0, 1), gfi_column(1, 1)),
        (gfi_line(0, 0, 0),),
        (gfi_line(0, 1, 0),),
        (gfi_line(1, 0, h - 1),),
        (gfi_line(1, 1, h - 1),),
    ]
    found = start(3, (2 * w, w), parts)
    for a in range(3):
        for b in range(3):
            total = None
            for p, q in phases:
                part = dot_in(view(x_feat, p + a - 1, q + b - 1), own_gfi[2 * p + q])
                total = part if total is None else total + part
            spread(parts_post, (3 * a + b) * chans, scale * total)
    post_1()
    post_2()
    middle()
    prior_1()
    prior_2()
    finish(found)
    for p in range(2):
        put(s_gfi(1), pl.ds(p * h * stride + EDGE - 1, h, stride=stride), halo(3, LEFT, p * h, h))
        put(s_gfi(0), pl.ds(p * h * stride + EDGE + w, h, stride=stride), halo(3, RIGHT, p * h, h))
        for q in range(2):
            x_gfi[p, 1 + q, p * w : p * w + cells, :] = own_gfi[2 * p + q]
            x_gfi[p, 1 + q, (1 - p) * cells : (1 - p) * cells + w, :] = halos[
                3, UP if p else DOWN, q * w : (q + 1) * w, :
            ]
        for i in range(h):
            here = slice((i + p) * w, (i + p + 1) * w)
            at = (i + p * h) * stride + EDGE
            x_gfi[p, 0, here, :] = get(s_gfi(1), pl.ds(at - 1, w)).astype(BF16)
            x_gfi[p, 3, here, :] = get(s_gfi(0), pl.ds(at + 1, w)).astype(BF16)
        ring_at = slice((1 - p) * cells, (1 - p) * cells + w)
        vertical_side = UP if p else DOWN
        left = halo(3, UP_LEFT if p else DOWN_LEFT, 0, w)[w - 1 :]
        right = halo(3, UP_RIGHT if p else DOWN_RIGHT, 0, w)[0:1]
        put(s_gfi(1), pl.ds(EDGE - 1, 1), left)
        put(s_gfi(1), pl.ds(EDGE, w), halo(3, vertical_side, w, w))
        put(s_gfi(0), pl.ds(EDGE, w), halo(3, vertical_side, 0, w))
        put(s_gfi(0), pl.ds(EDGE + w, 1), right)
        x_gfi[p, 0, ring_at, :] = get(s_gfi(1), pl.ds(EDGE - 1, w)).astype(BF16)
        x_gfi[p, 3, ring_at, :] = get(s_gfi(0), pl.ds(EDGE + 1, w)).astype(BF16)
    post_1()
    post_2()
    for p, q in phases:
        total = None
        for a in range(3):
            for b in range(3):
                part = dot_out(view(x_gfi, p - a + 1, q - b + 1), tap_of(w_post, a, b))
                total = part if total is None else total + part
        for i in range(h):
            put(mix, pl.ds((2 * i + p) * cols + q, w, stride=2), total[i * w : (i + 1) * w])
    grad_feat[...] = get(mix, pl.ds(0, rows * cols)).astype(BF16)
    for _ in range(bits + 1):
        for step in (prior_1, prior_2, middle, post_1, post_2):
            step()


def hand_out(*refs):
    for source, target in zip(refs[:4], refs[4:]):
        target[...] = source[...]


def on_device(sizes, feat, noise_fine, noise_coarse, w_post, w_coarse, w_prior):
    n_row, n_col = sizes
    rows, cols, chans = feat.shape
    h, w = rows // 2, cols // 2
    scale = 1.0 / math.sqrt(rows * n_row * cols * n_col)
    cells, quarter = rows * cols, h * w
    vmem = pl.BlockSpec(memory_space=pltpu.VMEM)
    dims = (rows, cols, chans, scale, n_row, n_col)
    count = n_row * n_col
    per = w_post.shape[0] // count
    widths = (chans // 2, chans // 2, chans, chans, chans)
    extra, side, stride = round_up(h + 1, 16), round_up(h + 2, 8), w + 2 * EDGE

    def lanes(n, depth=chans):
        return pltpu.VMEM((depth // LANES, n, LANES), F32)

    grad_feat, out_post, out_coarse, out_prior = pl.pallas_call(
        functools.partial(tile_kernel, dims),
        out_shape=(
            jax.ShapeDtypeStruct((cells, chans), BF16),
            jax.ShapeDtypeStruct((per * chans // LANES, LANES), F32),
            jax.ShapeDtypeStruct((per * chans // LANES, LANES), F32),
            jax.ShapeDtypeStruct((per * 2 * chans // LANES, LANES), F32),
        ),
        in_specs=[vmem] * 6,
        out_specs=(vmem,) * 4,
        scratch_shapes=[
            pltpu.VMEM((4, (h + 1) * w + extra, chans), F32),
            pltpu.VMEM((4, quarter, chans), F32),
            pltpu.VMEM((quarter, chans), F32),
            lanes((rows + 2) * (cols + 2 * EDGE)),
            lanes((side + 2) * stride),
            lanes(side * stride),
            lanes((extra + 1) * stride),
            pltpu.VMEM((2, 2 * chans // LANES, max(2 * h * stride, cells), LANES), F32),
            pltpu.VMEM((2, 4, (h + 1) * w, chans), BF16),
            pltpu.VMEM((3, (h + 4) * w, chans), BF16),
            pltpu.VMEM((9, 2 * side, chans), BF16),
            pltpu.VMEM((3, (h + 2) * w, chans), BF16),
            pltpu.VMEM((8, extra, chans), BF16),
            pltpu.VMEM((16, chans, 2 * chans), BF16),
            pltpu.VMEM((4, (h + 1) * w, 2 * chans), F32),
            pltpu.VMEM((4, extra, 2 * chans), F32),
            pltpu.VMEM((9, quarter, 2 * chans), BF16),
            pltpu.VMEM((4, quarter, chans), BF16),
            pltpu.VMEM((4, 8, 4 * w, chans), BF16),
            pltpu.VMEM((4, 8, 4 * w, chans), BF16),
            [pltpu.VMEM((count, per, width), F32) for width in widths],
            [pltpu.VMEM((count // 2, per, width), BF16) for width in widths],
            [pltpu.VMEM((count - 1, per, width), BF16) for width in widths],
            pltpu.SemaphoreType.DMA((4, 16)),
            pltpu.SemaphoreType.DMA((5, count.bit_length() - 1, 2)),
        ],
        compiler_params=pltpu.CompilerParams(
            collective_id=0, has_side_effects=True, vmem_limit_bytes=65000 * 1024
        ),
    )(
        feat.reshape(cells, chans),
        noise_fine.reshape(cells, chans),
        noise_coarse.reshape(quarter, chans),
        w_post,
        w_coarse,
        w_prior,
    )
    results = (grad_feat, out_post, out_coarse, out_prior)
    grad_feat, out_post, out_coarse, out_prior = pl.pallas_call(
        hand_out,
        out_shape=tuple(jax.ShapeDtypeStruct(a.shape, a.dtype) for a in results),
        in_specs=[vmem] * 4,
        out_specs=(vmem,) * 4,
    )(*results)
    return (
        grad_feat.reshape(rows, cols, chans),
        out_post.reshape(-1),
        out_coarse.reshape(-1),
        out_prior.reshape(-1),
    )


def solution(mesh):
    sizes = (mesh.shape["row"], mesh.shape["col"])
    return jax.shard_map(
        functools.partial(on_device, sizes),
        mesh=mesh,
        in_specs=(
            P("row", "col", None),
            P("row", "col", None),
            P("row", "col", None),
            P(),
            P(),
            P(),
        ),
        out_specs=(P("row", "col", None), P(("row", "col")), P(("row", "col")), P(("row", "col"))),
        check_vma=False,
    )
```

```python
import functools
import math

import jax
import jax.numpy as jnp
from jax import lax
from jax.experimental import pallas as pl
from jax.experimental.pallas import tpu as pltpu
from jax.sharding import PartitionSpec as P

F32 = jnp.float32
BF16 = jnp.bfloat16
EDGE = 8


LANES = 128


def put(ref, at, values):
    for d in range(values.shape[1] // LANES):
        ref[d, at, :] = values[:, d * LANES : (d + 1) * LANES]


def get(ref, at):
    return jnp.concatenate([ref[d, at, :] for d in range(ref.shape[0])], axis=1)


DIRECTIONS = ((-1, 0), (1, 0), (0, -1), (0, 1), (-1, -1), (-1, 1), (1, -1), (1, 1))
OPPOSITE = (1, 0, 3, 2, 7, 6, 5, 4)
UP, DOWN, LEFT, RIGHT, UP_LEFT, UP_RIGHT, DOWN_LEFT, DOWN_RIGHT = range(8)
CORNER = 16
TAPS = (((0,), (1, 2)), ((0, 1), (2,)))


def round_up(n, m):
    return -(-n // m) * m


def tile_kernel(
    dims,
    *refs,
):
    operands, results = refs[:6], refs[6:10]
    (
        feat,
        noise_fine,
        noise_coarse,
        w_post,
        w_coarse,
        w_prior,
        grad_feat,
        out_post,
        out_coarse,
        out_prior,
        fine,
        err,
        coarse,
        s_fine,
        s_pool,
        s_noise,
        s_ctx,
        s_pair,
        s_corner,
        x_feat,
        x_pool,
        side_pool,
        x_ctx,
        side_ctx,
        w_sums,
        g_main,
        g_side,
        boxes,
        own_gfi,
        edges,
        halos,
        sums,
        outgoing,
        incoming,
        sems,
        chain_sems,
        load_sems,
        store_sems,
    ) = refs[10:]
    loads = [
        pltpu.make_async_copy(source, target, load_sems.at[k])
        for k, (source, target) in enumerate(zip(operands, refs[10:16]))
    ]
    stores = [
        pltpu.make_async_copy(source, target, store_sems.at[k])
        for k, (source, target) in enumerate(zip(refs[16:20], results))
    ]
    for k in (0, 2, 5, 1, 3, 4):
        loads[k].start()
    x_gco, x_gfi = x_ctx, x_feat
    rows, cols, chans, scale, n_row, n_col, orders = dims
    mix = s_pair.at[0, pl.ds(0, chans // LANES)]
    h, w = rows // 2, cols // 2
    cells = h * w
    r = lax.axis_index("row")
    c = lax.axis_index("col")
    has_up, has_down = r > 0, r < n_row - 1
    has_left, has_right = c > 0, c < n_col - 1
    vertical = {-1: has_up, 0: None, 1: has_down}
    horizontal = {-1: has_left, 0: None, 1: has_right}

    def neighbour(d):
        down, right = DIRECTIONS[d]
        device = {}
        if down:
            device["row"] = r + down
        if right:
            device["col"] = c + right
        if not right:
            return vertical[down], device
        if not down:
            return horizontal[right], device
        return jnp.logical_and(vertical[down], horizontal[right]), device

    sides = [neighbour(d) for d in range(8)]

    halos[...] = jnp.zeros_like(halos)
    barrier = pltpu.get_barrier_semaphore()
    for has, device in sides:
        @pl.when(has)
        def _(device=device):
            pl.semaphore_signal(
                barrier, inc=1, device_id=device, device_id_type=pl.DeviceIdType.MESH
            )
    count = n_row * n_col
    bits = count.bit_length() - 1
    col_bits = n_col.bit_length() - 1
    me = r * n_col + c

    def bit_of(b):
        return me // 2**b % 2

    def reach(group, mask):
        row, col = r, c
        for q, b in enumerate(group):
            if mask >> q & 1:
                if b < col_bits:
                    col = col + 2**b * (1 - 2 * bit_of(b))
                else:
                    row = row + 2 ** (b - col_bits) * (1 - 2 * bit_of(b))
        return {"row": row, "col": col}

    partners = {}
    for order in orders:
        for group in order:
            for mask in range(1, 2 ** len(group)):
                flips = tuple(b for q, b in enumerate(group) if mask >> q & 1)
                partners[flips] = reach(group, mask)
    for device in partners.values():
        pl.semaphore_signal(
            barrier, inc=1, device_id=device, device_id_type=pl.DeviceIdType.MESH
        )

    for ref in (s_fine, s_pool, s_noise, s_ctx, s_corner, fine):
        ref[...] = jnp.zeros_like(ref)

    def enter():
        pl.semaphore_wait(barrier, len(partners) + sum(has.astype(jnp.int32) for has, _device in sides))

    def each(n, body):
        if n <= 16:
            for j in range(n):
                body(j)
        else:
            pl.loop(0, n)(body)

    def chain(number, order, out, out_at):
        acc, send, recv = sums[number], outgoing[number], incoming[number]
        state = {"step": 0, "copies": []}
        frees = [[b for b in range(bits) if b not in sum(order[:k], ())] for k in range(len(order) + 1)]
        lefts = [2 ** len(free) for free in frees]
        bases = [count - left for left in lefts]

        def arrived(k, slot):
            total = None
            for mask in range(1, 2 ** len(order[k])):
                part = recv[bases[k] + (mask - 1) * lefts[k + 1] + slot].astype(F32)
                total = part if total is None else total + part
            return total

        def step():
            k = state["step"]
            if k > len(order):
                return
            state["step"] = k + 1
            for copy in state["copies"]:
                copy.wait()
            state["copies"] = []
            if k == len(order):
                total = scale * (acc[me] + arrived(k - 1, 0))
                per = total.shape[0]
                stride = out.shape[0] // per
                for d in range(total.shape[1] // LANES):
                    out[pl.ds(out_at // LANES + d, per, stride=stride), :] = total[
                        :, d * LANES : (d + 1) * LANES
                    ]
                return
            group, free, n = order[k], frees[k], lefts[k + 1]
            rest = frees[k + 1]
            fixed = sum((bit_of(b) * 2**b for b in range(bits) if b not in free), 0)

            def value(j, mask):
                index, slot = fixed, 0
                for q, b in enumerate(free):
                    if b in group:
                        flip = mask >> group.index(b) & 1
                        bit = 1 - bit_of(b) if flip else bit_of(b)
                    else:
                        bit = j // 2 ** rest.index(b) % 2
                    index = index + bit * 2**b
                    slot = slot + bit * 2**q
                total = acc[index]
                if k > 0:
                    total = total + arrived(k - 1, slot)
                return index, total

            for mask in reversed(range(1, 2 ** len(group))):
                at = (mask - 1) * n

                def fill(j, mask=mask, at=at):
                    send[at + j] = value(j, mask)[1].astype(BF16)

                each(n, fill)
                copy = pltpu.make_async_remote_copy(
                    src_ref=send.at[pl.ds(at, n)],
                    dst_ref=recv.at[pl.ds(bases[k] + at, n)],
                    send_sem=chain_sems.at[number, k, mask - 1, 0],
                    recv_sem=chain_sems.at[number, k, mask - 1, 1],
                    device_id=reach(group, mask),
                    device_id_type=pl.DeviceIdType.MESH,
                )
                copy.start()
                state["copies"].append(copy)

            def keep(j):
                index, total = value(j, 0)
                acc[index] = total

            if k > 0:
                each(n, keep)

        return step


    pieces = chans // LANES
    post_chains = [chain(k, orders[k], out_post, k * LANES) for k in range(pieces)]
    middle_chains = [chain(k, orders[k], out_coarse, (k - pieces) * LANES) for k in range(pieces, 2 * pieces)]
    prior_chains = [
        chain(k, orders[k], out_prior, (k - 2 * pieces) * LANES)
        for k in range(2 * pieces, 4 * pieces)
    ]

    early, late = prior_chains[:2], prior_chains[2:]

    def advance(chains):
        for step in chains:
            step()

    parts_post = [(sums[k], k * LANES) for k in range(pieces)]
    parts_coarse = [(sums[k + pieces], k * LANES) for k in range(pieces)]
    parts_prior = [(sums[2 * pieces + k], k % pieces * LANES) for k in range(2 * pieces)]

    def spread(parts, start, values):
        height = values.shape[0]
        for acc, at in parts:
            per, width = acc.shape[1:]
            row = start
            while row < start + height:
                inner = row % per
                size = min(per - inner, start + height - row)
                acc[row // per, inner : inner + size] = values[
                    row - start : row - start + size, at : at + width
                ]
                row += size


    def copies(index, sizes):
        found = []
        for d in range(8):
            size = sizes[0] if d < 4 else sizes[1]
            found.append(
                pltpu.make_async_remote_copy(
                    src_ref=edges.at[index, d, pl.ds(0, size)],
                    dst_ref=halos.at[index, OPPOSITE[d], pl.ds(0, size)],
                    send_sem=sems.at[index, d],
                    recv_sem=sems.at[index, 8 + OPPOSITE[d]],
                    device_id=sides[d][1],
                    device_id_type=pl.DeviceIdType.MESH,
                )
            )
        return found

    def start(index, sizes, parts):
        found = copies(index, sizes)
        for d in (4, 5, 6, 7, 0, 1, 2, 3):
            at = 0
            for part in parts[d]:
                edges[index, d, at : at + part.shape[0], :] = part.astype(BF16)
                at += part.shape[0]
            pl.when(sides[d][0])(found[d].start)
        return found

    def finish(found):
        for d in range(8):
            @pl.when(sides[d][0])
            def _(d=d):
                found[d].wait_send()
                found[OPPOSITE[d]].wait_recv()

    def halo(index, d, at, size):
        return halos[index, d, at : at + size, :].astype(F32)

    def corner(k, *pieces):
        at = k * CORNER
        for piece in pieces:
            put(s_corner, pl.ds(at, piece.shape[0]), piece)
            at += piece.shape[0]
        return (get(s_corner, pl.ds(k * CORNER, CORNER)),)

    def view(x, t, u):
        return x[t % 2, u + 1, pl.ds(w if t >= 1 else 0, cells), :]

    def dot_in(x, g):
        return lax.dot_general(x, g, (((0,), (0,)), ((), ())), preferred_element_type=F32)

    def dot_out(g, weights):
        return lax.dot_general(g, weights, (((1,), (1,)), ((), ())), preferred_element_type=F32)

    def tap_of(weights, a, b):
        k = weights.shape[0] // 9
        return weights[(3 * a + b) * k : (3 * a + b + 1) * k, :]

    fine_stride = cols + 2 * EDGE
    stride = w + 2 * EDGE
    extra = round_up(h + 1, 16)
    side = round_up(h + 2, 8)
    phases = [(p, q) for p in range(2) for q in range(2)]

    loads[0].wait()
    loads[2].wait()
    for i in range(rows):
        put(
            s_fine,
            pl.ds((i + 1) * fine_stride + EDGE, cols),
            feat[pl.ds(i * cols, cols), :].astype(F32),
        )
    for i in range(h):
        put(s_noise, pl.ds((i + 1) * stride + EDGE, w), noise_coarse[pl.ds(i * w, w), :])
    top, bottom = feat[0:cols, :], feat[(rows - 1) * cols :, :]
    noise_top, noise_bottom = noise_coarse[0:w, :], noise_coarse[(h - 1) * w :, :]
    parts = [
        (top, noise_top),
        (bottom, noise_bottom),
        (
            get(s_fine, pl.ds(fine_stride + EDGE, rows, stride=fine_stride)),
            get(s_noise, pl.ds(stride + EDGE, h, stride=stride)),
        ),
        (
            get(s_fine, pl.ds(fine_stride + EDGE + cols - 1, rows, stride=fine_stride)),
            get(s_noise, pl.ds(stride + EDGE + w - 1, h, stride=stride)),
        ),
    ]
    for k in range(4):
        i, j = k // 2, k % 2
        at = (i * (rows - 1) + 1) * fine_stride + EDGE + j * (cols - 1)
        noise_at = (i * (h - 1) + 1) * stride + EDGE + j * (w - 1)
        parts.append(corner(k, get(s_fine, pl.ds(at, 1)), get(s_noise, pl.ds(noise_at, 1))))
    enter()
    found = start(0, (cols + w, CORNER), parts)

    loads[5].wait()
    for p, q in phases:
        for kr in range(2):
            for kc in range(2):
                total = None
                for a in TAPS[p][kr]:
                    for b in TAPS[q][kc]:
                        part = tap_of(w_prior, a, b).astype(F32)
                        total = part if total is None else total + part
                w_sums[((2 * p + kr) * 2 + q) * 2 + kc] = total.astype(BF16)

    def own(p):
        return slice(p * w, p * w + cells)

    loads[1].wait()
    put(mix, pl.ds(0, rows * cols), noise_fine[...])
    for p, q in phases:
        for i in range(h):
            fine[2 * p + q, (i + p) * w : (i + p + 1) * w, :] = get(
                mix, pl.ds((2 * i + p) * cols + q, w, stride=2)
            )

    def fill_feat(i, ms):
        p = i % 2
        at = (i - p) // 2 + p
        for m in ms:
            x_feat[p, m, at * w : (at + 1) * w, :] = get(
                s_fine, pl.ds((i + 1) * fine_stride + EDGE - 1 + m, w, stride=2)
            ).astype(BF16)

    for i in range(rows):
        fill_feat(i, (1, 2))
    def dot_fine(p, q, a, b):
        x = view(x_feat, p + a - 1, q + b - 1)
        return jnp.dot(x, tap_of(w_post, a, b), preferred_element_type=F32)

    loads[3].wait()
    for p, q in phases:
        total = None
        for a in range(1 - p, 3 - p):
            for b in range(1 - q, 3 - q):
                part = dot_fine(p, q, a, b)
                total = part if total is None else total + part
        fine[2 * p + q, own(p), :] = total + fine[2 * p + q, own(p), :]
    finish(found)
    put(s_fine, pl.ds(EDGE, cols), halo(0, UP, 0, cols))
    put(s_fine, pl.ds((rows + 1) * fine_stride + EDGE, cols), halo(0, DOWN, 0, cols))
    put(s_fine, pl.ds(fine_stride + EDGE - 1, rows, stride=fine_stride), halo(0, LEFT, 0, rows))
    put(s_fine, pl.ds(fine_stride + EDGE + cols, rows, stride=fine_stride), halo(0, RIGHT, 0, rows))
    put(s_fine, pl.ds(EDGE - 1, 1), halo(0, UP_LEFT, 0, CORNER)[0:1])
    put(s_fine, pl.ds(EDGE + cols, 1), halo(0, UP_RIGHT, 0, CORNER)[0:1])
    last = (rows + 1) * fine_stride + EDGE
    put(s_fine, pl.ds(last - 1, 1), halo(0, DOWN_LEFT, 0, CORNER)[0:1])
    put(s_fine, pl.ds(last + cols, 1), halo(0, DOWN_RIGHT, 0, CORNER)[0:1])
    for i in range(rows):
        fill_feat(i, (0, 3))
    fill_feat(-1, (0, 1, 2, 3))
    fill_feat(rows, (0, 1, 2, 3))

    pooled = None
    for p, q in phases:
        total = None
        for a in range(3):
            for b in range(3):
                if p + a - 1 in (0, 1) and q + b - 1 in (0, 1):
                    continue
                part = dot_fine(p, q, a, b)
                total = part if total is None else total + part
        total = total + fine[2 * p + q, own(p), :]
        fine[2 * p + q, own(p), :] = total
        pooled = total if pooled is None else pooled + total
    pooled = (0.25 * pooled).astype(BF16).astype(F32)
    for i in range(h):
        put(s_pool, pl.ds((i + 2) * stride + EDGE, w), pooled[i * w : (i + 1) * w])

    def line(p, q, i):
        return fine[2 * p + q, (i + p) * w : (i + p + 1) * w, :]

    def column(values, j):
        put(mix, pl.ds(0, cells), values)
        return get(mix, pl.ds(j, h, stride=w))

    pool_top, pool_bottom = pooled[0 : 2 * w], pooled[(h - 2) * w :]

    def pool_column(j):
        return get(s_pool, pl.ds(2 * stride + EDGE + j, h, stride=stride))

    lefts = [column(fine[2 * p, own(p), :], 0) for p in range(2)]
    rights = [column(fine[2 * p + 1, own(p), :], w - 1) for p in range(2)]
    parts = [
        (pool_top, line(0, 0, 0), line(0, 1, 0)),
        (pool_bottom, line(1, 0, h - 1), line(1, 1, h - 1)),
        (pool_column(0), pool_column(1), *lefts),
        (pool_column(w - 2), pool_column(w - 1), *rights),
    ]
    for k in range(4):
        i, j = k // 2, k % 2
        at = (i * (h - 2) + 2) * stride + EDGE + j * (w - 2)
        cell = line(i, j, i * (h - 1))[j * (w - 1) : j * (w - 1) + 1]
        parts.append(
            corner(k, get(s_pool, pl.ds(at, 2)), get(s_pool, pl.ds(at + stride, 2)), cell)
        )
    found = start(1, (4 * w, CORNER), parts)
    for i in range(h):
        put(s_noise, pl.ds((i + 1) * stride + EDGE, w), noise_coarse[pl.ds(i * w, w), :])
    put(s_noise, pl.ds(EDGE, w), halo(0, UP, cols, w))
    put(s_noise, pl.ds((h + 1) * stride + EDGE, w), halo(0, DOWN, cols, w))
    put(s_noise, pl.ds(stride + EDGE - 1, h, stride=stride), halo(0, LEFT, rows, h))
    put(s_noise, pl.ds(stride + EDGE + w, h, stride=stride), halo(0, RIGHT, rows, h))
    put(s_noise, pl.ds(EDGE - 1, 1), halo(0, UP_LEFT, 0, CORNER)[1:2])
    put(s_noise, pl.ds(EDGE + w, 1), halo(0, UP_RIGHT, 0, CORNER)[1:2])
    last = (h + 1) * stride + EDGE
    put(s_noise, pl.ds(last - 1, 1), halo(0, DOWN_LEFT, 0, CORNER)[1:2])
    put(s_noise, pl.ds(last + w, 1), halo(0, DOWN_RIGHT, 0, CORNER)[1:2])
    finish(found)
    for k in range(2):
        put(s_pool, pl.ds(k * stride + EDGE, w), halo(1, UP, k * w, w))
        put(s_pool, pl.ds((h + 2 + k) * stride + EDGE, w), halo(1, DOWN, k * w, w))
        put(s_pool, pl.ds(2 * stride + EDGE - 2 + k, h, stride=stride), halo(1, LEFT, k * h, h))
        put(s_pool, pl.ds(2 * stride + EDGE + w + k, h, stride=stride), halo(1, RIGHT, k * h, h))
        put(s_pool, pl.ds(k * stride + EDGE - 2, 2), halo(1, UP_LEFT, 0, CORNER)[2 * k : 2 * k + 2])
        put(s_pool, pl.ds(k * stride + EDGE + w, 2), halo(1, UP_RIGHT, 0, CORNER)[2 * k : 2 * k + 2])
        at = (h + 2 + k) * stride + EDGE
        put(s_pool, pl.ds(at - 2, 2), halo(1, DOWN_LEFT, 0, CORNER)[2 * k : 2 * k + 2])
        put(s_pool, pl.ds(at + w, 2), halo(1, DOWN_RIGHT, 0, CORNER)[2 * k : 2 * k + 2])
    base = cells + w
    for q in range(2):
        fine[q, cells : cells + w, :] = halo(1, DOWN, (2 + q) * w, w)
        fine[2 + q, 0:w, :] = halo(1, UP, (2 + q) * w, w)
    for p in range(2):
        fine[2 * p, base + p : base + p + h, :] = halo(1, RIGHT, (2 + p) * h, h)
        fine[2 * p + 1, base + p : base + p + h, :] = halo(1, LEFT, (2 + p) * h, h)
    fine[3, base : base + 1, :] = halo(1, UP_LEFT, 0, CORNER)[4:5]
    fine[2, base : base + 1, :] = halo(1, UP_RIGHT, 0, CORNER)[4:5]
    fine[1, base + h : base + h + 1, :] = halo(1, DOWN_LEFT, 0, CORNER)[4:5]
    fine[0, base + h : base + h + 1, :] = halo(1, DOWN_RIGHT, 0, CORNER)[4:5]

    loads[4].wait()
    for i in range(h + 4):
        for b in range(3):
            x_pool[b, i * w : (i + 1) * w, :] = get(
                s_pool, pl.ds(i * stride + EDGE + b - 1, w)
            ).astype(BF16)
    for a in range(3):
        for b in range(3):
            both = [
                get(s_pool, pl.ds(a * stride + EDGE - 2 + b, side, stride=stride)),
                get(s_pool, pl.ds(a * stride + EDGE + w - 1 + b, side, stride=stride)),
            ]
            side_pool[3 * a + b] = jnp.concatenate(both, axis=0).astype(BF16)
    ring = (h + 2) * w
    noise = jnp.concatenate(
        [get(s_noise, pl.ds(i * stride + EDGE, w)) for i in range(h + 2)]
        + [
            get(s_noise, pl.ds(EDGE - 1, side, stride=stride)),
            get(s_noise, pl.ds(EDGE + w, side, stride=stride)),
        ],
        axis=0,
    )
    total = None
    for a in range(3):
        for b in range(3):
            x = jnp.concatenate([x_pool[b, pl.ds(a * w, ring), :], side_pool[3 * a + b]], axis=0)
            part = jnp.dot(x, tap_of(w_coarse, a, b), preferred_element_type=F32)
            total = part if total is None else total + part
    total = total + noise
    coarse[...] = total[w : w + cells]
    total = total.astype(BF16).astype(F32)
    put(s_ctx, pl.ds(EDGE, w), jnp.where(has_up, total[0:w], 0.0))
    for i in range(1, h + 1):
        put(s_ctx, pl.ds(i * stride + EDGE, w), total[i * w : (i + 1) * w])
    put(s_ctx, pl.ds((h + 1) * stride + EDGE, w), jnp.where(has_down, total[ring - w : ring], 0.0))
    place = lax.broadcasted_iota(jnp.int32, (side, chans), 0)
    first = jnp.where(has_up, 0, 1)
    limit = jnp.where(has_down, h + 2, h + 1)
    inside = jnp.logical_and(place >= first, place < limit)
    for at, has, values in (
        (EDGE - 1, has_left, total[ring : ring + side]),
        (EDGE + w, has_right, total[ring + side :]),
    ):
        put(
            s_ctx,
            pl.ds(at, side, stride=stride),
            jnp.where(jnp.logical_and(inside, has), values, 0.0),
        )
    for i in range(h + 2):
        for k in range(3):
            x_ctx[k, i * w : (i + 1) * w, :] = get(
                s_ctx, pl.ds(i * stride + EDGE + k - 1, w)
            ).astype(BF16)
    for q in range(2):
        for kr in range(2):
            for kc in range(2):
                at = kr * stride + EDGE + (w - 1 if q == 0 else -1) + kc
                side_ctx[(2 * q + kr) * 2 + kc] = get(
                    s_ctx, pl.ds(at, extra, stride=stride)
                ).astype(BF16)

    place = lax.broadcasted_iota(jnp.int32, (extra, 2 * chans), 0)
    for p, q in phases:
        prior = None
        for kr in range(2):
            for kc in range(2):
                x = jnp.concatenate(
                    [x_ctx[q + kc, pl.ds(kr * w, base), :], side_ctx[(2 * q + kr) * 2 + kc]],
                    axis=0,
                )
                part = jnp.dot(
                    x, w_sums[((2 * p + kr) * 2 + q) * 2 + kc], preferred_element_type=F32
                )
                prior = part if prior is None else prior + part
        raw = prior[:, chans:]
        small = jnp.exp(-jnp.abs(raw))
        sigma = jnp.maximum(raw, 0.0) + jnp.log1p(small) + 0.5
        gate = jnp.where(raw >= 0, 1.0, small) / (1.0 + small)
        inverse = 1.0 / sigma
        ratio = (fine[2 * p + q] - prior[:, :chans]) * inverse
        residual = ratio * inverse
        err[2 * p + q] = residual[own(p)]
        slope = (inverse - ratio * ratio * inverse) * gate
        both = jnp.concatenate([-residual, slope], axis=1).astype(BF16).astype(F32)
        if p == 0:
            g_main[q, 0:cells, :] = both[0:cells]
            g_main[q, cells:, :] = jnp.where(has_down, both[cells:base], 0.0)
            inside = jnp.logical_or(has_down, place < h)
        else:
            g_main[2 + q, 0:w, :] = jnp.where(has_up, both[0:w], 0.0)
            g_main[2 + q, w:, :] = both[w:base]
            inside = jnp.logical_or(has_up, place > 0)
        inside = jnp.logical_and(inside, has_left if q else has_right)
        g_side[2 * p + q] = jnp.where(inside, both[base:], 0.0)

    windows = ((1, 1), (0, 1), (0, 0))
    for a in range(3):
        i0, i1 = windows[a]
        for q in range(2):
            total = g_main[q, pl.ds(i0 * w, cells), :] + g_main[2 + q, pl.ds(i1 * w, cells), :]
            for i in range(h):
                put(s_pair.at[q], pl.ds(i * stride + EDGE, w), total[i * w : (i + 1) * w])
            total = g_side[q, i0 : i0 + h, :] + g_side[2 + q, i1 : i1 + h, :]
            put(s_pair.at[q], pl.ds(EDGE - 1 if q else EDGE + w, h, stride=stride), total)
        for i in range(h):
            at = i * stride + EDGE
            even, odd = get(s_pair.at[0], pl.ds(at, w)), get(s_pair.at[1], pl.ds(at, w))
            here = slice(i * w, (i + 1) * w)
            boxes[3 * a, here, :] = (odd + get(s_pair.at[0], pl.ds(at + 1, w))).astype(BF16)
            boxes[3 * a + 1, here, :] = (even + odd).astype(BF16)
            boxes[3 * a + 2, here, :] = (get(s_pair.at[1], pl.ds(at - 1, w)) + even).astype(BF16)

    total = None
    for tap in range(9):
        part = dot_out(boxes[tap], tap_of(w_prior, tap // 3, tap % 3))
        total = part if total is None else total + part
    total = (coarse[...] + total).astype(BF16).astype(F32)

    def pad_lines(values):
        for i in range(h):
            put(s_pool, pl.ds((i + 1) * stride + EDGE, w), values[i * w : (i + 1) * w])

    pad_lines(total)
    parts = [
        (total[0:w],),
        (total[cells - w :],),
        (get(s_pool, pl.ds(stride + EDGE, h, stride=stride)),),
        (get(s_pool, pl.ds(stride + EDGE + w - 1, h, stride=stride)),),
    ]
    for k in range(4):
        i, j = k // 2, k % 2
        at = (i * (h - 1) + 1) * stride + EDGE + j * (w - 1)
        parts.append(corner(k, get(s_pool, pl.ds(at, 1))))
    found = start(2, (w, CORNER), parts)
    for part in range(2):
        for tap in range(9):
            spread(
                parts_prior[2 * part : 2 * part + 2],
                tap * chans,
                dot_in(
                    x_ctx[1, pl.ds(w, cells), :], boxes[tap, :, part * chans : (part + 1) * chans]
                ),
            )
        advance(prior_chains[2 * part : 2 * part + 2])
    gco = total.astype(BF16)
    for a in range(3):
        for b in range(3):
            spread(
                parts_coarse,
                (3 * a + b) * chans,
                dot_in(x_pool[b, pl.ds((a + 1) * w, cells), :], gco),
            )
    advance(early)
    advance(middle_chains)
    advance(late)
    advance(middle_chains)
    finish(found)

    put(s_pool, pl.ds(EDGE, w), halo(2, UP, 0, w))
    put(s_pool, pl.ds((h + 1) * stride + EDGE, w), halo(2, DOWN, 0, w))
    put(s_pool, pl.ds(stride + EDGE - 1, h, stride=stride), halo(2, LEFT, 0, h))
    put(s_pool, pl.ds(stride + EDGE + w, h, stride=stride), halo(2, RIGHT, 0, h))
    put(s_pool, pl.ds(EDGE - 1, 1), halo(2, UP_LEFT, 0, CORNER)[0:1])
    put(s_pool, pl.ds(EDGE + w, 1), halo(2, UP_RIGHT, 0, CORNER)[0:1])
    last = (h + 1) * stride + EDGE
    put(s_pool, pl.ds(last - 1, 1), halo(2, DOWN_LEFT, 0, CORNER)[0:1])
    put(s_pool, pl.ds(last + w, 1), halo(2, DOWN_RIGHT, 0, CORNER)[0:1])
    for i in range(h + 2):
        for k in range(3):
            x_gco[k, i * w : (i + 1) * w, :] = get(
                s_pool, pl.ds(i * stride + EDGE + k - 1, w)
            ).astype(BF16)
    total = None
    for a in range(3):
        for b in range(3):
            part = dot_out(x_gco[2 - b, pl.ds((2 - a) * w, cells), :], tap_of(w_coarse, a, b))
            total = part if total is None else total + part
    total = 0.25 * total

    for p, q in phases:
        own_gfi[2 * p + q] = (err[2 * p + q] + total).astype(BF16)

    def s_gfi(q):
        return s_pair.at[q, pl.ds(0, chans // LANES)]

    def gfi_line(p, q, i):
        return own_gfi[2 * p + q, i * w : (i + 1) * w, :]

    for p, q in phases:
        for i in range(h):
            put(
                s_gfi(q),
                pl.ds((i + p * h) * stride + EDGE, w),
                own_gfi[2 * p + q, i * w : (i + 1) * w, :].astype(F32),
            )

    def gfi_column(p, q):
        at = p * h * stride + EDGE + (w - 1 if q else 0)
        return get(s_gfi(q), pl.ds(at, h, stride=stride))

    parts = [
        (gfi_line(0, 0, 0), gfi_line(0, 1, 0)),
        (gfi_line(1, 0, h - 1), gfi_line(1, 1, h - 1)),
        (gfi_column(0, 0), gfi_column(1, 0)),
        (gfi_column(0, 1), gfi_column(1, 1)),
    ]
    for k in range(4):
        i, j = k // 2, k % 2
        at = i * (2 * h - 1) * stride + EDGE + j * (w - 1)
        parts.append(corner(k, get(s_gfi(j), pl.ds(at, 1))))
    found = start(3, (2 * w, CORNER), parts)
    for a in range(3):
        for b in range(3):
            total = None
            for p, q in phases:
                part = dot_in(view(x_feat, p + a - 1, q + b - 1), own_gfi[2 * p + q])
                total = part if total is None else total + part
            spread(parts_post, (3 * a + b) * chans, total)
    advance(post_chains)
    advance(post_chains)
    advance(prior_chains)
    advance(middle_chains)
    finish(found)
    for p in range(2):
        put(s_gfi(1), pl.ds(p * h * stride + EDGE - 1, h, stride=stride), halo(3, LEFT, p * h, h))
        put(s_gfi(0), pl.ds(p * h * stride + EDGE + w, h, stride=stride), halo(3, RIGHT, p * h, h))
        for q in range(2):
            x_gfi[p, 1 + q, p * w : p * w + cells, :] = own_gfi[2 * p + q]
            x_gfi[p, 1 + q, (1 - p) * cells : (1 - p) * cells + w, :] = halos[
                3, UP if p else DOWN, q * w : (q + 1) * w, :
            ]
        for i in range(h):
            here = slice((i + p) * w, (i + p + 1) * w)
            at = (i + p * h) * stride + EDGE
            x_gfi[p, 0, here, :] = get(s_gfi(1), pl.ds(at - 1, w)).astype(BF16)
            x_gfi[p, 3, here, :] = get(s_gfi(0), pl.ds(at + 1, w)).astype(BF16)
        ring_at = slice((1 - p) * cells, (1 - p) * cells + w)
        vertical_side = UP if p else DOWN
        left = halo(3, UP_LEFT if p else DOWN_LEFT, 0, CORNER)[0:1]
        right = halo(3, UP_RIGHT if p else DOWN_RIGHT, 0, CORNER)[0:1]
        put(s_gfi(1), pl.ds(EDGE - 1, 1), left)
        put(s_gfi(1), pl.ds(EDGE, w), halo(3, vertical_side, w, w))
        put(s_gfi(0), pl.ds(EDGE, w), halo(3, vertical_side, 0, w))
        put(s_gfi(0), pl.ds(EDGE + w, 1), right)
        x_gfi[p, 0, ring_at, :] = get(s_gfi(1), pl.ds(EDGE - 1, w)).astype(BF16)
        x_gfi[p, 3, ring_at, :] = get(s_gfi(0), pl.ds(EDGE + 1, w)).astype(BF16)
    for p, q in phases:
        total = None
        for a in range(3):
            for b in range(3):
                part = dot_out(view(x_gfi, p - a + 1, q - b + 1), tap_of(w_post, a, b))
                total = part if total is None else total + part
        for i in range(h):
            put(mix, pl.ds((2 * i + p) * cols + q, w, stride=2), total[i * w : (i + 1) * w])
    grad_feat[...] = get(mix, pl.ds(0, rows * cols)).astype(BF16)
    stores[0].start()
    advance(post_chains)
    advance(prior_chains)
    advance(middle_chains)
    advance(post_chains)
    advance(prior_chains)
    advance(middle_chains)
    for _ in range(bits):
        advance(prior_chains + middle_chains + post_chains)
    for store in stores[1:]:
        store.start()
    for store in stores:
        store.wait()


def hand_out(*refs):
    for source, target in zip(refs[:4], refs[4:]):
        target[...] = source[...]


def orders_of(n_row, n_col, pieces):
    bits = (n_row * n_col).bit_length() - 1
    near, a, b = (0,), 1, n_col.bit_length() - 1
    far = [k for k in range(1, bits) if k not in (a, b)]
    pairs = [tuple(far[k : k + 2]) for k in range(0, len(far), 2)]
    singles = [(k,) for k in far]
    post = (near, (a, b), *pairs)
    middle = (near, singles[0], (a, b), *singles[1:])
    prior = ((near, (b,), (a,), *pairs), (near, (a,), (b,), *pairs))
    return (post,) * pieces + (middle,) * pieces + prior * pieces


def on_device(sizes, feat, noise_fine, noise_coarse, w_post, w_coarse, w_prior):
    n_row, n_col = sizes
    rows, cols, chans = feat.shape
    h, w = rows // 2, cols // 2
    scale = 1.0 / math.sqrt(rows * n_row * cols * n_col)
    cells, quarter = rows * cols, h * w
    vmem = pl.BlockSpec(memory_space=pltpu.VMEM)
    count = n_row * n_col
    orders = orders_of(n_row, n_col, chans // LANES)
    dims = (rows, cols, chans, scale, n_row, n_col, orders)
    per = w_post.shape[0] // count
    widths = (LANES,) * len(orders)
    anywhere = pl.BlockSpec(memory_space=pl.ANY)
    extra, side, stride = round_up(h + 1, 16), round_up(h + 2, 8), w + 2 * EDGE

    def lanes(n, depth=chans):
        return pltpu.VMEM((depth // LANES, n, LANES), F32)

    grad_feat, out_post, out_coarse, out_prior = pl.pallas_call(
        functools.partial(tile_kernel, dims),
        out_shape=(
            jax.ShapeDtypeStruct((cells, chans), BF16),
            jax.ShapeDtypeStruct((per * chans // LANES, LANES), F32),
            jax.ShapeDtypeStruct((per * chans // LANES, LANES), F32),
            jax.ShapeDtypeStruct((per * 2 * chans // LANES, LANES), F32),
        ),
        in_specs=[anywhere] * 6,
        out_specs=(anywhere,) * 4,
        scratch_shapes=[
            pltpu.VMEM((cells, chans), BF16),
            pltpu.VMEM((cells, chans), F32),
            pltpu.VMEM((quarter, chans), F32),
            pltpu.VMEM(w_post.shape, BF16),
            pltpu.VMEM(w_coarse.shape, BF16),
            pltpu.VMEM(w_prior.shape, BF16),
            pltpu.VMEM((cells, chans), BF16),
            pltpu.VMEM((per * chans // LANES, LANES), F32),
            pltpu.VMEM((per * chans // LANES, LANES), F32),
            pltpu.VMEM((per * 2 * chans // LANES, LANES), F32),
            pltpu.VMEM((4, (h + 1) * w + extra, chans), F32),
            pltpu.VMEM((4, quarter, chans), F32),
            pltpu.VMEM((quarter, chans), F32),
            lanes((rows + 2) * (cols + 2 * EDGE)),
            lanes((side + 2) * stride),
            lanes(side * stride),
            lanes((extra + 1) * stride),
            pltpu.VMEM((2, 2 * chans // LANES, max(2 * h * stride, cells), LANES), F32),
            lanes(4 * CORNER),
            pltpu.VMEM((2, 4, (h + 1) * w, chans), BF16),
            pltpu.VMEM((3, (h + 4) * w, chans), BF16),
            pltpu.VMEM((9, 2 * side, chans), BF16),
            pltpu.VMEM((3, (h + 2) * w, chans), BF16),
            pltpu.VMEM((8, extra, chans), BF16),
            pltpu.VMEM((16, chans, 2 * chans), BF16),
            pltpu.VMEM((4, (h + 1) * w, 2 * chans), F32),
            pltpu.VMEM((4, extra, 2 * chans), F32),
            pltpu.VMEM((9, quarter, 2 * chans), BF16),
            pltpu.VMEM((4, quarter, chans), BF16),
            pltpu.VMEM((4, 8, 4 * w, chans), BF16),
            pltpu.VMEM((4, 8, 4 * w, chans), BF16),
            [pltpu.VMEM((count, per, width), F32) for width in widths],
            [pltpu.VMEM((count // 2, per, width), BF16) for width in widths],
            [pltpu.VMEM((count - 1, per, width), BF16) for width in widths],
            pltpu.SemaphoreType.DMA((4, 16)),
            pltpu.SemaphoreType.DMA((len(orders), max(map(len, orders)), 3, 2)),
            pltpu.SemaphoreType.DMA((6,)),
            pltpu.SemaphoreType.DMA((4,)),
        ],
        compiler_params=pltpu.CompilerParams(
            collective_id=0, has_side_effects=True, vmem_limit_bytes=65000 * 1024
        ),
    )(
        feat.reshape(cells, chans),
        noise_fine.reshape(cells, chans),
        noise_coarse.reshape(quarter, chans),
        w_post,
        w_coarse,
        w_prior,
    )
    results = (grad_feat, out_post, out_coarse, out_prior)
    grad_feat, out_post, out_coarse, out_prior = pl.pallas_call(
        hand_out,
        out_shape=tuple(jax.ShapeDtypeStruct(a.shape, a.dtype) for a in results),
        in_specs=[vmem] * 4,
        out_specs=(vmem,) * 4,
    )(*results)
    return (
        grad_feat.reshape(rows, cols, chans),
        out_post.reshape(-1),
        out_coarse.reshape(-1),
        out_prior.reshape(-1),
    )


def solution(mesh):
    sizes = (mesh.shape["row"], mesh.shape["col"])
    return jax.shard_map(
        functools.partial(on_device, sizes),
        mesh=mesh,
        in_specs=(
            P("row", "col", None),
            P("row", "col", None),
            P("row", "col", None),
            P(),
            P(),
            P(),
        ),
        out_specs=(P("row", "col", None), P(("row", "col")), P(("row", "col")), P(("row", "col"))),
        check_vma=False,
    )
```

```python
import functools
import math

import jax
import jax.numpy as jnp
from jax import lax
from jax.experimental import pallas as pl
from jax.experimental.pallas import tpu as pltpu
from jax.sharding import PartitionSpec as P

F32 = jnp.float32
BF16 = jnp.bfloat16
EDGE = 8


LANES = 128


def put(ref, at, values):
    for d in range(values.shape[1] // LANES):
        ref[d, at, :] = values[:, d * LANES : (d + 1) * LANES]


def get(ref, at):
    return jnp.concatenate([ref[d, at, :] for d in range(ref.shape[0])], axis=1)


DIRECTIONS = ((-1, 0), (1, 0), (0, -1), (0, 1), (-1, -1), (-1, 1), (1, -1), (1, 1))
OPPOSITE = (1, 0, 3, 2, 7, 6, 5, 4)
UP, DOWN, LEFT, RIGHT, UP_LEFT, UP_RIGHT, DOWN_LEFT, DOWN_RIGHT = range(8)
CORNER = 16
TAPS = (((0,), (1, 2)), ((0, 1), (2,)))


def round_up(n, m):
    return -(-n // m) * m


def tile_kernel(
    dims,
    *refs,
):
    operands = refs[:6]
    grad_feat, out_post, out_coarse, out_prior = refs[6:10]
    (
        feat,
        noise_fine,
        noise_coarse,
        w_post,
        w_coarse,
        w_prior,
        fine,
        err,
        coarse,
        s_fine,
        s_pool,
        s_noise,
        s_ctx,
        s_pair,
        s_corner,
        x_feat,
        x_pool,
        side_pool,
        x_ctx,
        side_ctx,
        w_sums,
        g_main,
        g_side,
        boxes,
        own_gfi,
        edges,
        halos,
        sums,
        outgoing,
        incoming,
        sems,
        chain_sems,
        load_sems,
    ) = refs[10:]
    loads = [
        pltpu.make_async_copy(source, target, load_sems.at[k])
        for k, (source, target) in enumerate(zip(operands, refs[10:16]))
    ]
    for k in (0, 2, 5, 1, 3, 4):
        loads[k].start()
    x_gco, x_gfi = x_ctx, x_feat
    rows, cols, chans, scale, n_row, n_col, orders = dims
    mix = s_pair.at[0, pl.ds(0, chans // LANES)]
    h, w = rows // 2, cols // 2
    cells = h * w
    r = lax.axis_index("row")
    c = lax.axis_index("col")
    has_up, has_down = r > 0, r < n_row - 1
    has_left, has_right = c > 0, c < n_col - 1
    vertical = {-1: has_up, 0: None, 1: has_down}
    horizontal = {-1: has_left, 0: None, 1: has_right}

    def neighbour(d):
        down, right = DIRECTIONS[d]
        device = {}
        if down:
            device["row"] = r + down
        if right:
            device["col"] = c + right
        if not right:
            return vertical[down], device
        if not down:
            return horizontal[right], device
        return jnp.logical_and(vertical[down], horizontal[right]), device

    sides = [neighbour(d) for d in range(8)]

    halos[...] = jnp.zeros_like(halos)
    barrier = pltpu.get_barrier_semaphore()
    for has, device in sides:
        @pl.when(has)
        def _(device=device):
            pl.semaphore_signal(
                barrier, inc=1, device_id=device, device_id_type=pl.DeviceIdType.MESH
            )
    count = n_row * n_col
    bits = count.bit_length() - 1
    col_bits = n_col.bit_length() - 1
    me = r * n_col + c

    def bit_of(b):
        return me // 2**b % 2

    def reach(group, mask):
        row, col = r, c
        for q, b in enumerate(group):
            if mask >> q & 1:
                if b < col_bits:
                    col = col + 2**b * (1 - 2 * bit_of(b))
                else:
                    row = row + 2 ** (b - col_bits) * (1 - 2 * bit_of(b))
        return {"row": row, "col": col}

    partners = {}
    for order in orders:
        for group in order:
            for mask in range(1, 2 ** len(group)):
                flips = tuple(b for q, b in enumerate(group) if mask >> q & 1)
                partners[flips] = reach(group, mask)
    for device in partners.values():
        pl.semaphore_signal(
            barrier, inc=1, device_id=device, device_id_type=pl.DeviceIdType.MESH
        )

    for ref in (s_fine, s_pool, s_noise, s_ctx, s_corner, fine):
        ref[...] = jnp.zeros_like(ref)

    def enter():
        pl.semaphore_wait(barrier, len(partners) + sum(has.astype(jnp.int32) for has, _device in sides))

    def each(n, body):
        if n <= 16:
            for j in range(n):
                body(j)
        else:
            pl.loop(0, n)(body)

    def chain(number, order, out, out_at):
        acc, send, recv = sums[number], outgoing[number], incoming[number]
        state = {"step": 0, "copies": []}
        frees = [[b for b in range(bits) if b not in sum(order[:k], ())] for k in range(len(order) + 1)]
        lefts = [2 ** len(free) for free in frees]
        bases = [count - left for left in lefts]

        def arrived(k, slot):
            total = None
            for mask in range(1, 2 ** len(order[k])):
                part = recv[bases[k] + (mask - 1) * lefts[k + 1] + slot].astype(F32)
                total = part if total is None else total + part
            return total

        def begin(half):
            n = lefts[1] // 2
            at = half * n
            other = 1 - bit_of(order[0][0])

            def fill(j):
                send[at + j] = acc[2 * (at + j) + other].astype(BF16)

            each(n, fill)
            copy = pltpu.make_async_remote_copy(
                src_ref=send.at[pl.ds(at, n)],
                dst_ref=recv.at[pl.ds(at, n)],
                send_sem=chain_sems.at[number, 0, half, 0],
                recv_sem=chain_sems.at[number, 0, half, 1],
                device_id=reach(order[0], 1),
                device_id_type=pl.DeviceIdType.MESH,
            )
            copy.start()
            state["copies"].append(copy)
            state["step"] = 1

        def step():
            k = state["step"]
            if k > len(order):
                return
            state["step"] = k + 1
            for copy in state["copies"]:
                copy.wait()
            state["copies"] = []
            if k == len(order):
                total = scale * (acc[me] + arrived(k - 1, 0))
                per = total.shape[0]
                stride = out.shape[0] // per
                for d in range(total.shape[1] // LANES):
                    out[pl.ds(out_at // LANES + d, per, stride=stride), :] = total[
                        :, d * LANES : (d + 1) * LANES
                    ]
                return
            group, free, n = order[k], frees[k], lefts[k + 1]
            rest = frees[k + 1]
            fixed = sum((bit_of(b) * 2**b for b in range(bits) if b not in free), 0)

            def value(j, mask):
                index, slot = fixed, 0
                for q, b in enumerate(free):
                    if b in group:
                        flip = mask >> group.index(b) & 1
                        bit = 1 - bit_of(b) if flip else bit_of(b)
                    else:
                        bit = j // 2 ** rest.index(b) % 2
                    index = index + bit * 2**b
                    slot = slot + bit * 2**q
                total = acc[index]
                if k > 0:
                    total = total + arrived(k - 1, slot)
                return index, total

            for mask in reversed(range(1, 2 ** len(group))):
                at = (mask - 1) * n

                def fill(j, mask=mask, at=at):
                    send[at + j] = value(j, mask)[1].astype(BF16)

                each(n, fill)
                copy = pltpu.make_async_remote_copy(
                    src_ref=send.at[pl.ds(at, n)],
                    dst_ref=recv.at[pl.ds(bases[k] + at, n)],
                    send_sem=chain_sems.at[number, k, mask - 1, 0],
                    recv_sem=chain_sems.at[number, k, mask - 1, 1],
                    device_id=reach(group, mask),
                    device_id_type=pl.DeviceIdType.MESH,
                )
                copy.start()
                state["copies"].append(copy)

            def keep(j):
                index, total = value(j, 0)
                acc[index] = total

            if k > 0:
                each(n, keep)

        return step, begin


    pieces = chans // LANES
    post_chains = [chain(k, orders[k], out_post, k * LANES) for k in range(pieces)]
    middle_chains = [chain(k, orders[k], out_coarse, (k - pieces) * LANES) for k in range(pieces, 2 * pieces)]
    prior_chains = [
        chain(k, orders[k], out_prior, (k - 2 * pieces) * LANES)
        for k in range(2 * pieces, 4 * pieces)
    ]

    early, late = prior_chains[:2], prior_chains[2:]

    def advance(chains):
        for step, _begin in chains:
            step()

    def begin(chains, tap):
        if tap in (4, 8):
            for _step, start_half in chains:
                start_half(tap // 8)

    parts_post = [(sums[k], k * LANES) for k in range(pieces)]
    parts_coarse = [(sums[k + pieces], k * LANES) for k in range(pieces)]
    parts_prior = [(sums[2 * pieces + k], k % pieces * LANES) for k in range(2 * pieces)]

    def spread(parts, start, values):
        height = values.shape[0]
        for acc, at in parts:
            per, width = acc.shape[1:]
            row = start
            while row < start + height:
                inner = row % per
                size = min(per - inner, start + height - row)
                acc[row // per, inner : inner + size] = values[
                    row - start : row - start + size, at : at + width
                ]
                row += size


    def copies(index, sizes):
        found = []
        for d in range(8):
            size = sizes[0] if d < 4 else sizes[1]
            found.append(
                pltpu.make_async_remote_copy(
                    src_ref=edges.at[index, d, pl.ds(0, size)],
                    dst_ref=halos.at[index, OPPOSITE[d], pl.ds(0, size)],
                    send_sem=sems.at[index, d],
                    recv_sem=sems.at[index, 8 + OPPOSITE[d]],
                    device_id=sides[d][1],
                    device_id_type=pl.DeviceIdType.MESH,
                )
            )
        return found

    def start(index, sizes, parts):
        found = copies(index, sizes)
        for d in (4, 5, 6, 7, 0, 1, 2, 3):
            at = 0
            for part in parts[d]:
                edges[index, d, at : at + part.shape[0], :] = part.astype(BF16)
                at += part.shape[0]
            pl.when(sides[d][0])(found[d].start)
        return found

    def finish(found):
        for d in range(8):
            @pl.when(sides[d][0])
            def _(d=d):
                found[d].wait_send()
                found[OPPOSITE[d]].wait_recv()

    def halo(index, d, at, size):
        return halos[index, d, at : at + size, :].astype(F32)

    def corner(k, *pieces):
        at = k * CORNER
        for piece in pieces:
            put(s_corner, pl.ds(at, piece.shape[0]), piece)
            at += piece.shape[0]
        return (get(s_corner, pl.ds(k * CORNER, CORNER)),)

    def view(x, t, u):
        return x[t % 2, u + 1, pl.ds(w if t >= 1 else 0, cells), :]

    def dot_in(x, g):
        return lax.dot_general(x, g, (((0,), (0,)), ((), ())), preferred_element_type=F32)

    def dot_out(g, weights):
        return lax.dot_general(g, weights, (((1,), (1,)), ((), ())), preferred_element_type=F32)

    def tap_of(weights, a, b):
        k = weights.shape[0] // 9
        return weights[(3 * a + b) * k : (3 * a + b + 1) * k, :]

    fine_stride = cols + 2 * EDGE
    stride = w + 2 * EDGE
    extra = round_up(h + 1, 16)
    side = round_up(h + 2, 8)
    phases = [(p, q) for p in range(2) for q in range(2)]

    loads[0].wait()
    loads[2].wait()
    for i in range(rows):
        put(
            s_fine,
            pl.ds((i + 1) * fine_stride + EDGE, cols),
            feat[pl.ds(i * cols, cols), :].astype(F32),
        )
    for i in range(h):
        put(s_noise, pl.ds((i + 1) * stride + EDGE, w), noise_coarse[pl.ds(i * w, w), :])
    top, bottom = feat[0:cols, :], feat[(rows - 1) * cols :, :]
    noise_top, noise_bottom = noise_coarse[0:w, :], noise_coarse[(h - 1) * w :, :]
    parts = [
        (top, noise_top),
        (bottom, noise_bottom),
        (
            get(s_fine, pl.ds(fine_stride + EDGE, rows, stride=fine_stride)),
            get(s_noise, pl.ds(stride + EDGE, h, stride=stride)),
        ),
        (
            get(s_fine, pl.ds(fine_stride + EDGE + cols - 1, rows, stride=fine_stride)),
            get(s_noise, pl.ds(stride + EDGE + w - 1, h, stride=stride)),
        ),
    ]
    for k in range(4):
        i, j = k // 2, k % 2
        at = (i * (rows - 1) + 1) * fine_stride + EDGE + j * (cols - 1)
        noise_at = (i * (h - 1) + 1) * stride + EDGE + j * (w - 1)
        parts.append(corner(k, get(s_fine, pl.ds(at, 1)), get(s_noise, pl.ds(noise_at, 1))))
    enter()
    found = start(0, (cols + w, CORNER), parts)

    loads[5].wait()
    for p, q in phases:
        for kr in range(2):
            for kc in range(2):
                total = None
                for a in TAPS[p][kr]:
                    for b in TAPS[q][kc]:
                        part = tap_of(w_prior, a, b).astype(F32)
                        total = part if total is None else total + part
                w_sums[((2 * p + kr) * 2 + q) * 2 + kc] = total.astype(BF16)

    def own(p):
        return slice(p * w, p * w + cells)

    loads[1].wait()
    put(mix, pl.ds(0, rows * cols), noise_fine[...])
    for p, q in phases:
        for i in range(h):
            fine[2 * p + q, (i + p) * w : (i + p + 1) * w, :] = get(
                mix, pl.ds((2 * i + p) * cols + q, w, stride=2)
            )

    def fill_feat(i, ms):
        p = i % 2
        at = (i - p) // 2 + p
        for m in ms:
            x_feat[p, m, at * w : (at + 1) * w, :] = get(
                s_fine, pl.ds((i + 1) * fine_stride + EDGE - 1 + m, w, stride=2)
            ).astype(BF16)

    for i in range(rows):
        fill_feat(i, (1, 2))
    def dot_fine(p, q, a, b):
        x = view(x_feat, p + a - 1, q + b - 1)
        return jnp.dot(x, tap_of(w_post, a, b), preferred_element_type=F32)

    loads[3].wait()
    for p, q in phases:
        total = None
        for a in range(1 - p, 3 - p):
            for b in range(1 - q, 3 - q):
                part = dot_fine(p, q, a, b)
                total = part if total is None else total + part
        fine[2 * p + q, own(p), :] = total + fine[2 * p + q, own(p), :]
    finish(found)
    put(s_fine, pl.ds(EDGE, cols), halo(0, UP, 0, cols))
    put(s_fine, pl.ds((rows + 1) * fine_stride + EDGE, cols), halo(0, DOWN, 0, cols))
    put(s_fine, pl.ds(fine_stride + EDGE - 1, rows, stride=fine_stride), halo(0, LEFT, 0, rows))
    put(s_fine, pl.ds(fine_stride + EDGE + cols, rows, stride=fine_stride), halo(0, RIGHT, 0, rows))
    put(s_fine, pl.ds(EDGE - 1, 1), halo(0, UP_LEFT, 0, CORNER)[0:1])
    put(s_fine, pl.ds(EDGE + cols, 1), halo(0, UP_RIGHT, 0, CORNER)[0:1])
    last = (rows + 1) * fine_stride + EDGE
    put(s_fine, pl.ds(last - 1, 1), halo(0, DOWN_LEFT, 0, CORNER)[0:1])
    put(s_fine, pl.ds(last + cols, 1), halo(0, DOWN_RIGHT, 0, CORNER)[0:1])
    for i in range(rows):
        fill_feat(i, (0, 3))
    fill_feat(-1, (0, 1, 2, 3))
    fill_feat(rows, (0, 1, 2, 3))

    pooled = None
    for p, q in phases:
        total = None
        for a in range(3):
            for b in range(3):
                if p + a - 1 in (0, 1) and q + b - 1 in (0, 1):
                    continue
                part = dot_fine(p, q, a, b)
                total = part if total is None else total + part
        total = total + fine[2 * p + q, own(p), :]
        fine[2 * p + q, own(p), :] = total
        pooled = total if pooled is None else pooled + total
    pooled = (0.25 * pooled).astype(BF16).astype(F32)
    for i in range(h):
        put(s_pool, pl.ds((i + 2) * stride + EDGE, w), pooled[i * w : (i + 1) * w])

    def line(p, q, i):
        return fine[2 * p + q, (i + p) * w : (i + p + 1) * w, :]

    def column(values, j):
        put(mix, pl.ds(0, cells), values)
        return get(mix, pl.ds(j, h, stride=w))

    pool_top, pool_bottom = pooled[0 : 2 * w], pooled[(h - 2) * w :]

    def pool_column(j):
        return get(s_pool, pl.ds(2 * stride + EDGE + j, h, stride=stride))

    lefts = [column(fine[2 * p, own(p), :], 0) for p in range(2)]
    rights = [column(fine[2 * p + 1, own(p), :], w - 1) for p in range(2)]
    parts = [
        (pool_top, line(0, 0, 0), line(0, 1, 0)),
        (pool_bottom, line(1, 0, h - 1), line(1, 1, h - 1)),
        (pool_column(0), pool_column(1), *lefts),
        (pool_column(w - 2), pool_column(w - 1), *rights),
    ]
    for k in range(4):
        i, j = k // 2, k % 2
        at = (i * (h - 2) + 2) * stride + EDGE + j * (w - 2)
        cell = line(i, j, i * (h - 1))[j * (w - 1) : j * (w - 1) + 1]
        parts.append(
            corner(k, get(s_pool, pl.ds(at, 2)), get(s_pool, pl.ds(at + stride, 2)), cell)
        )
    found = start(1, (4 * w, CORNER), parts)
    for i in range(h):
        put(s_noise, pl.ds((i + 1) * stride + EDGE, w), noise_coarse[pl.ds(i * w, w), :])
    put(s_noise, pl.ds(EDGE, w), halo(0, UP, cols, w))
    put(s_noise, pl.ds((h + 1) * stride + EDGE, w), halo(0, DOWN, cols, w))
    put(s_noise, pl.ds(stride + EDGE - 1, h, stride=stride), halo(0, LEFT, rows, h))
    put(s_noise, pl.ds(stride + EDGE + w, h, stride=stride), halo(0, RIGHT, rows, h))
    put(s_noise, pl.ds(EDGE - 1, 1), halo(0, UP_LEFT, 0, CORNER)[1:2])
    put(s_noise, pl.ds(EDGE + w, 1), halo(0, UP_RIGHT, 0, CORNER)[1:2])
    last = (h + 1) * stride + EDGE
    put(s_noise, pl.ds(last - 1, 1), halo(0, DOWN_LEFT, 0, CORNER)[1:2])
    put(s_noise, pl.ds(last + w, 1), halo(0, DOWN_RIGHT, 0, CORNER)[1:2])
    finish(found)
    for k in range(2):
        put(s_pool, pl.ds(k * stride + EDGE, w), halo(1, UP, k * w, w))
        put(s_pool, pl.ds((h + 2 + k) * stride + EDGE, w), halo(1, DOWN, k * w, w))
        put(s_pool, pl.ds(2 * stride + EDGE - 2 + k, h, stride=stride), halo(1, LEFT, k * h, h))
        put(s_pool, pl.ds(2 * stride + EDGE + w + k, h, stride=stride), halo(1, RIGHT, k * h, h))
        put(s_pool, pl.ds(k * stride + EDGE - 2, 2), halo(1, UP_LEFT, 0, CORNER)[2 * k : 2 * k + 2])
        put(s_pool, pl.ds(k * stride + EDGE + w, 2), halo(1, UP_RIGHT, 0, CORNER)[2 * k : 2 * k + 2])
        at = (h + 2 + k) * stride + EDGE
        put(s_pool, pl.ds(at - 2, 2), halo(1, DOWN_LEFT, 0, CORNER)[2 * k : 2 * k + 2])
        put(s_pool, pl.ds(at + w, 2), halo(1, DOWN_RIGHT, 0, CORNER)[2 * k : 2 * k + 2])
    base = cells + w
    for q in range(2):
        fine[q, cells : cells + w, :] = halo(1, DOWN, (2 + q) * w, w)
        fine[2 + q, 0:w, :] = halo(1, UP, (2 + q) * w, w)
    for p in range(2):
        fine[2 * p, base + p : base + p + h, :] = halo(1, RIGHT, (2 + p) * h, h)
        fine[2 * p + 1, base + p : base + p + h, :] = halo(1, LEFT, (2 + p) * h, h)
    fine[3, base : base + 1, :] = halo(1, UP_LEFT, 0, CORNER)[4:5]
    fine[2, base : base + 1, :] = halo(1, UP_RIGHT, 0, CORNER)[4:5]
    fine[1, base + h : base + h + 1, :] = halo(1, DOWN_LEFT, 0, CORNER)[4:5]
    fine[0, base + h : base + h + 1, :] = halo(1, DOWN_RIGHT, 0, CORNER)[4:5]

    loads[4].wait()
    for i in range(h + 4):
        for b in range(3):
            x_pool[b, i * w : (i + 1) * w, :] = get(
                s_pool, pl.ds(i * stride + EDGE + b - 1, w)
            ).astype(BF16)
    for a in range(3):
        for b in range(3):
            both = [
                get(s_pool, pl.ds(a * stride + EDGE - 2 + b, side, stride=stride)),
                get(s_pool, pl.ds(a * stride + EDGE + w - 1 + b, side, stride=stride)),
            ]
            side_pool[3 * a + b] = jnp.concatenate(both, axis=0).astype(BF16)
    ring = (h + 2) * w
    noise = jnp.concatenate(
        [get(s_noise, pl.ds(i * stride + EDGE, w)) for i in range(h + 2)]
        + [
            get(s_noise, pl.ds(EDGE - 1, side, stride=stride)),
            get(s_noise, pl.ds(EDGE + w, side, stride=stride)),
        ],
        axis=0,
    )
    total = None
    for a in range(3):
        for b in range(3):
            x = jnp.concatenate([x_pool[b, pl.ds(a * w, ring), :], side_pool[3 * a + b]], axis=0)
            part = jnp.dot(x, tap_of(w_coarse, a, b), preferred_element_type=F32)
            total = part if total is None else total + part
    total = total + noise
    coarse[...] = total[w : w + cells]
    total = total.astype(BF16).astype(F32)
    put(s_ctx, pl.ds(EDGE, w), jnp.where(has_up, total[0:w], 0.0))
    for i in range(1, h + 1):
        put(s_ctx, pl.ds(i * stride + EDGE, w), total[i * w : (i + 1) * w])
    put(s_ctx, pl.ds((h + 1) * stride + EDGE, w), jnp.where(has_down, total[ring - w : ring], 0.0))
    place = lax.broadcasted_iota(jnp.int32, (side, chans), 0)
    first = jnp.where(has_up, 0, 1)
    limit = jnp.where(has_down, h + 2, h + 1)
    inside = jnp.logical_and(place >= first, place < limit)
    for at, has, values in (
        (EDGE - 1, has_left, total[ring : ring + side]),
        (EDGE + w, has_right, total[ring + side :]),
    ):
        put(
            s_ctx,
            pl.ds(at, side, stride=stride),
            jnp.where(jnp.logical_and(inside, has), values, 0.0),
        )
    for i in range(h + 2):
        for k in range(3):
            x_ctx[k, i * w : (i + 1) * w, :] = get(
                s_ctx, pl.ds(i * stride + EDGE + k - 1, w)
            ).astype(BF16)
    for q in range(2):
        for kr in range(2):
            for kc in range(2):
                at = kr * stride + EDGE + (w - 1 if q == 0 else -1) + kc
                side_ctx[(2 * q + kr) * 2 + kc] = get(
                    s_ctx, pl.ds(at, extra, stride=stride)
                ).astype(BF16)

    place = lax.broadcasted_iota(jnp.int32, (extra, 2 * chans), 0)
    for p, q in phases:
        prior = None
        for kr in range(2):
            for kc in range(2):
                x = jnp.concatenate(
                    [x_ctx[q + kc, pl.ds(kr * w, base), :], side_ctx[(2 * q + kr) * 2 + kc]],
                    axis=0,
                )
                part = jnp.dot(
                    x, w_sums[((2 * p + kr) * 2 + q) * 2 + kc], preferred_element_type=F32
                )
                prior = part if prior is None else prior + part
        raw = prior[:, chans:]
        small = jnp.exp(-jnp.abs(raw))
        sigma = jnp.maximum(raw, 0.0) + jnp.log1p(small) + 0.5
        whole = 1.0 + small
        both_inverse = 1.0 / (sigma * whole)
        gate = jnp.where(raw >= 0, 1.0, small) * (sigma * both_inverse)
        inverse = whole * both_inverse
        ratio = (fine[2 * p + q] - prior[:, :chans]) * inverse
        residual = ratio * inverse
        err[2 * p + q] = residual[own(p)]
        slope = (inverse - ratio * ratio * inverse) * gate
        both = jnp.concatenate([-residual, slope], axis=1).astype(BF16).astype(F32)
        if p == 0:
            g_main[q, 0:cells, :] = both[0:cells]
            g_main[q, cells:, :] = jnp.where(has_down, both[cells:base], 0.0)
            inside = jnp.logical_or(has_down, place < h)
        else:
            g_main[2 + q, 0:w, :] = jnp.where(has_up, both[0:w], 0.0)
            g_main[2 + q, w:, :] = both[w:base]
            inside = jnp.logical_or(has_up, place > 0)
        inside = jnp.logical_and(inside, has_left if q else has_right)
        g_side[2 * p + q] = jnp.where(inside, both[base:], 0.0)

    windows = ((1, 1), (0, 1), (0, 0))
    for a in range(3):
        i0, i1 = windows[a]
        for q in range(2):
            total = g_main[q, pl.ds(i0 * w, cells), :] + g_main[2 + q, pl.ds(i1 * w, cells), :]
            for i in range(h):
                put(s_pair.at[q], pl.ds(i * stride + EDGE, w), total[i * w : (i + 1) * w])
            total = g_side[q, i0 : i0 + h, :] + g_side[2 + q, i1 : i1 + h, :]
            put(s_pair.at[q], pl.ds(EDGE - 1 if q else EDGE + w, h, stride=stride), total)
        for i in range(h):
            at = i * stride + EDGE
            even, odd = get(s_pair.at[0], pl.ds(at, w)), get(s_pair.at[1], pl.ds(at, w))
            here = slice(i * w, (i + 1) * w)
            boxes[3 * a, here, :] = (odd + get(s_pair.at[0], pl.ds(at + 1, w))).astype(BF16)
            boxes[3 * a + 1, here, :] = (even + odd).astype(BF16)
            boxes[3 * a + 2, here, :] = (get(s_pair.at[1], pl.ds(at - 1, w)) + even).astype(BF16)

    total = None
    for tap in range(9):
        part = dot_out(boxes[tap], tap_of(w_prior, tap // 3, tap % 3))
        total = part if total is None else total + part
    total = (coarse[...] + total).astype(BF16).astype(F32)

    def pad_lines(values):
        for i in range(h):
            put(s_pool, pl.ds((i + 1) * stride + EDGE, w), values[i * w : (i + 1) * w])

    pad_lines(total)
    parts = [
        (total[0:w],),
        (total[cells - w :],),
        (get(s_pool, pl.ds(stride + EDGE, h, stride=stride)),),
        (get(s_pool, pl.ds(stride + EDGE + w - 1, h, stride=stride)),),
    ]
    for k in range(4):
        i, j = k // 2, k % 2
        at = (i * (h - 1) + 1) * stride + EDGE + j * (w - 1)
        parts.append(corner(k, get(s_pool, pl.ds(at, 1))))
    found = start(2, (w, CORNER), parts)
    for part in range(2):
        for tap in range(9):
            spread(
                parts_prior[2 * part : 2 * part + 2],
                tap * chans,
                dot_in(
                    x_ctx[1, pl.ds(w, cells), :], boxes[tap, :, part * chans : (part + 1) * chans]
                ),
            )
            begin(prior_chains[2 * part : 2 * part + 2], tap)
    gco = total.astype(BF16)
    for a in range(3):
        for b in range(3):
            spread(
                parts_coarse,
                (3 * a + b) * chans,
                dot_in(x_pool[b, pl.ds((a + 1) * w, cells), :], gco),
            )
            begin(middle_chains, 3 * a + b)
    advance(early)
    advance(late)
    advance(middle_chains)
    finish(found)

    put(s_pool, pl.ds(EDGE, w), halo(2, UP, 0, w))
    put(s_pool, pl.ds((h + 1) * stride + EDGE, w), halo(2, DOWN, 0, w))
    put(s_pool, pl.ds(stride + EDGE - 1, h, stride=stride), halo(2, LEFT, 0, h))
    put(s_pool, pl.ds(stride + EDGE + w, h, stride=stride), halo(2, RIGHT, 0, h))
    put(s_pool, pl.ds(EDGE - 1, 1), halo(2, UP_LEFT, 0, CORNER)[0:1])
    put(s_pool, pl.ds(EDGE + w, 1), halo(2, UP_RIGHT, 0, CORNER)[0:1])
    last = (h + 1) * stride + EDGE
    put(s_pool, pl.ds(last - 1, 1), halo(2, DOWN_LEFT, 0, CORNER)[0:1])
    put(s_pool, pl.ds(last + w, 1), halo(2, DOWN_RIGHT, 0, CORNER)[0:1])
    for i in range(h + 2):
        for k in range(3):
            x_gco[k, i * w : (i + 1) * w, :] = get(
                s_pool, pl.ds(i * stride + EDGE + k - 1, w)
            ).astype(BF16)
    total = None
    for a in range(3):
        for b in range(3):
            part = dot_out(x_gco[2 - b, pl.ds((2 - a) * w, cells), :], tap_of(w_coarse, a, b))
            total = part if total is None else total + part
    total = 0.25 * total

    for p, q in phases:
        own_gfi[2 * p + q] = (err[2 * p + q] + total).astype(BF16)

    def s_gfi(q):
        return s_pair.at[q, pl.ds(0, chans // LANES)]

    def gfi_line(p, q, i):
        return own_gfi[2 * p + q, i * w : (i + 1) * w, :]

    for p, q in phases:
        for i in range(h):
            put(
                s_gfi(q),
                pl.ds((i + p * h) * stride + EDGE, w),
                own_gfi[2 * p + q, i * w : (i + 1) * w, :].astype(F32),
            )

    def gfi_column(p, q):
        at = p * h * stride + EDGE + (w - 1 if q else 0)
        return get(s_gfi(q), pl.ds(at, h, stride=stride))

    parts = [
        (gfi_line(0, 0, 0), gfi_line(0, 1, 0)),
        (gfi_line(1, 0, h - 1), gfi_line(1, 1, h - 1)),
        (gfi_column(0, 0), gfi_column(1, 0)),
        (gfi_column(0, 1), gfi_column(1, 1)),
    ]
    for k in range(4):
        i, j = k // 2, k % 2
        at = i * (2 * h - 1) * stride + EDGE + j * (w - 1)
        parts.append(corner(k, get(s_gfi(j), pl.ds(at, 1))))
    found = start(3, (2 * w, CORNER), parts)
    for a in range(3):
        for b in range(3):
            total = None
            for p, q in phases:
                part = dot_in(view(x_feat, p + a - 1, q + b - 1), own_gfi[2 * p + q])
                total = part if total is None else total + part
            spread(parts_post, (3 * a + b) * chans, total)
            begin(post_chains, 3 * a + b)
    advance(post_chains)
    advance(prior_chains)
    advance(middle_chains)
    finish(found)
    for p in range(2):
        put(s_gfi(1), pl.ds(p * h * stride + EDGE - 1, h, stride=stride), halo(3, LEFT, p * h, h))
        put(s_gfi(0), pl.ds(p * h * stride + EDGE + w, h, stride=stride), halo(3, RIGHT, p * h, h))
        for q in range(2):
            x_gfi[p, 1 + q, p * w : p * w + cells, :] = own_gfi[2 * p + q]
            x_gfi[p, 1 + q, (1 - p) * cells : (1 - p) * cells + w, :] = halos[
                3, UP if p else DOWN, q * w : (q + 1) * w, :
            ]
        for i in range(h):
            here = slice((i + p) * w, (i + p + 1) * w)
            at = (i + p * h) * stride + EDGE
            x_gfi[p, 0, here, :] = get(s_gfi(1), pl.ds(at - 1, w)).astype(BF16)
            x_gfi[p, 3, here, :] = get(s_gfi(0), pl.ds(at + 1, w)).astype(BF16)
        ring_at = slice((1 - p) * cells, (1 - p) * cells + w)
        vertical_side = UP if p else DOWN
        left = halo(3, UP_LEFT if p else DOWN_LEFT, 0, CORNER)[0:1]
        right = halo(3, UP_RIGHT if p else DOWN_RIGHT, 0, CORNER)[0:1]
        put(s_gfi(1), pl.ds(EDGE - 1, 1), left)
        put(s_gfi(1), pl.ds(EDGE, w), halo(3, vertical_side, w, w))
        put(s_gfi(0), pl.ds(EDGE, w), halo(3, vertical_side, 0, w))
        put(s_gfi(0), pl.ds(EDGE + w, 1), right)
        x_gfi[p, 0, ring_at, :] = get(s_gfi(1), pl.ds(EDGE - 1, w)).astype(BF16)
        x_gfi[p, 3, ring_at, :] = get(s_gfi(0), pl.ds(EDGE + 1, w)).astype(BF16)
    for p, q in phases:
        total = None
        for a in range(3):
            for b in range(3):
                part = dot_out(view(x_gfi, p - a + 1, q - b + 1), tap_of(w_post, a, b))
                total = part if total is None else total + part
        for i in range(h):
            put(mix, pl.ds((2 * i + p) * cols + q, w, stride=2), total[i * w : (i + 1) * w])
    grad_feat[...] = get(mix, pl.ds(0, rows * cols)).astype(BF16)
    advance(post_chains)
    advance(prior_chains)
    advance(middle_chains)
    advance(post_chains)
    advance(prior_chains)
    advance(middle_chains)
    for _ in range(bits):
        advance(prior_chains + middle_chains + post_chains)


def hand_out(*refs):
    for source, target in zip(refs[:4], refs[4:]):
        target[...] = source[...]


def orders_of(n_row, n_col, pieces):
    bits = (n_row * n_col).bit_length() - 1
    near, a, b = (0,), 1, n_col.bit_length() - 1
    far = [k for k in range(1, bits) if k not in (a, b)]
    pairs = [tuple(far[k : k + 2]) for k in range(0, len(far), 2)]
    singles = [(k,) for k in far]
    post = (near, (a, b), *pairs)
    middle = (near, singles[0], (a, b), *singles[1:])
    prior = ((near, (b,), (a,), *pairs), (near, (a,), (b,), *pairs))
    return (post,) * pieces + (middle,) * pieces + prior * pieces


def on_device(sizes, feat, noise_fine, noise_coarse, w_post, w_coarse, w_prior):
    n_row, n_col = sizes
    rows, cols, chans = feat.shape
    h, w = rows // 2, cols // 2
    scale = 1.0 / math.sqrt(rows * n_row * cols * n_col)
    cells, quarter = rows * cols, h * w
    vmem = pl.BlockSpec(memory_space=pltpu.VMEM)
    count = n_row * n_col
    orders = orders_of(n_row, n_col, chans // LANES)
    dims = (rows, cols, chans, scale, n_row, n_col, orders)
    per = w_post.shape[0] // count
    widths = (LANES,) * len(orders)
    anywhere = pl.BlockSpec(memory_space=pl.ANY)
    extra, side, stride = round_up(h + 1, 16), round_up(h + 2, 8), w + 2 * EDGE

    def lanes(n, depth=chans):
        return pltpu.VMEM((depth // LANES, n, LANES), F32)

    grad_feat, out_post, out_coarse, out_prior = pl.pallas_call(
        functools.partial(tile_kernel, dims),
        out_shape=(
            pltpu.VMEM((cells, chans), BF16),
            pltpu.VMEM((per * chans // LANES, LANES), F32),
            pltpu.VMEM((per * chans // LANES, LANES), F32),
            pltpu.VMEM((per * 2 * chans // LANES, LANES), F32),
        ),
        in_specs=[anywhere] * 6,
        out_specs=(vmem,) * 4,
        scratch_shapes=[
            pltpu.VMEM((cells, chans), BF16),
            pltpu.VMEM((cells, chans), F32),
            pltpu.VMEM((quarter, chans), F32),
            pltpu.VMEM(w_post.shape, BF16),
            pltpu.VMEM(w_coarse.shape, BF16),
            pltpu.VMEM(w_prior.shape, BF16),
            pltpu.VMEM((4, (h + 1) * w + extra, chans), F32),
            pltpu.VMEM((4, quarter, chans), F32),
            pltpu.VMEM((quarter, chans), F32),
            lanes((rows + 2) * (cols + 2 * EDGE)),
            lanes((side + 2) * stride),
            lanes(side * stride),
            lanes((extra + 1) * stride),
            pltpu.VMEM((2, 2 * chans // LANES, max(2 * h * stride, cells), LANES), F32),
            lanes(4 * CORNER),
            pltpu.VMEM((2, 4, (h + 1) * w, chans), BF16),
            pltpu.VMEM((3, (h + 4) * w, chans), BF16),
            pltpu.VMEM((9, 2 * side, chans), BF16),
            pltpu.VMEM((3, (h + 2) * w, chans), BF16),
            pltpu.VMEM((8, extra, chans), BF16),
            pltpu.VMEM((16, chans, 2 * chans), BF16),
            pltpu.VMEM((4, (h + 1) * w, 2 * chans), F32),
            pltpu.VMEM((4, extra, 2 * chans), F32),
            pltpu.VMEM((9, quarter, 2 * chans), BF16),
            pltpu.VMEM((4, quarter, chans), BF16),
            pltpu.VMEM((4, 8, 4 * w, chans), BF16),
            pltpu.VMEM((4, 8, 4 * w, chans), BF16),
            [pltpu.VMEM((count, per, width), F32) for width in widths],
            [pltpu.VMEM((count // 2, per, width), BF16) for width in widths],
            [pltpu.VMEM((count - 1, per, width), BF16) for width in widths],
            pltpu.SemaphoreType.DMA((4, 16)),
            pltpu.SemaphoreType.DMA((len(orders), max(map(len, orders)), 3, 2)),
            pltpu.SemaphoreType.DMA((6,)),
        ],
        compiler_params=pltpu.CompilerParams(
            collective_id=0, has_side_effects=True, vmem_limit_bytes=62 * 2**20
        ),
    )(
        feat.reshape(cells, chans),
        noise_fine.reshape(cells, chans),
        noise_coarse.reshape(quarter, chans),
        w_post,
        w_coarse,
        w_prior,
    )
    results = tuple(
        pltpu.with_memory_space_constraint(a, pltpu.VMEM)
        for a in (grad_feat, out_post, out_coarse, out_prior)
    )
    grad_feat, out_post, out_coarse, out_prior = pl.pallas_call(
        hand_out,
        out_shape=tuple(jax.ShapeDtypeStruct(a.shape, a.dtype) for a in results),
        in_specs=[vmem] * 4,
        out_specs=(vmem,) * 4,
    )(*results)
    return (
        grad_feat.reshape(rows, cols, chans),
        out_post.reshape(-1),
        out_coarse.reshape(-1),
        out_prior.reshape(-1),
    )


def solution(mesh):
    sizes = (mesh.shape["row"], mesh.shape["col"])
    return jax.shard_map(
        functools.partial(on_device, sizes),
        mesh=mesh,
        in_specs=(
            P("row", "col", None),
            P("row", "col", None),
            P("row", "col", None),
            P(),
            P(),
            P(),
        ),
        out_specs=(P("row", "col", None), P(("row", "col")), P(("row", "col")), P(("row", "col"))),
        check_vma=False,
    )
```

```python
import functools
import math

import jax
import jax.numpy as jnp
from jax import lax
from jax.experimental import pallas as pl
from jax.experimental.pallas import tpu as pltpu
from jax.sharding import PartitionSpec as P

F32 = jnp.float32
BF16 = jnp.bfloat16
EDGE = 8


LANES = 128


def put(ref, at, values):
    for d in range(values.shape[1] // LANES):
        ref[d, at, :] = values[:, d * LANES : (d + 1) * LANES]


def get(ref, at):
    return jnp.concatenate([ref[d, at, :] for d in range(ref.shape[0])], axis=1)


DIRECTIONS = ((-1, 0), (1, 0), (0, -1), (0, 1), (-1, -1), (-1, 1), (1, -1), (1, 1))
OPPOSITE = (1, 0, 3, 2, 7, 6, 5, 4)
UP, DOWN, LEFT, RIGHT, UP_LEFT, UP_RIGHT, DOWN_LEFT, DOWN_RIGHT = range(8)
CORNER = 16
TAPS = (((0,), (1, 2)), ((0, 1), (2,)))


def round_up(n, m):
    return -(-n // m) * m


def tile_kernel(
    dims,
    *refs,
):
    operands = refs[:6]
    grad_feat, out_post, out_coarse, out_prior = refs[6:10]
    (
        feat,
        noise_fine,
        noise_coarse,
        w_post,
        w_coarse,
        w_prior,
        fine,
        err,
        coarse,
        s_fine,
        s_pool,
        s_noise,
        s_ctx,
        s_pair,
        s_corner,
        x_feat,
        x_pool,
        side_pool,
        x_ctx,
        side_ctx,
        w_sums,
        g_main,
        g_side,
        boxes,
        own_gfi,
        edges,
        halos,
        sums,
        outgoing,
        incoming,
        sems,
        chain_sems,
        load_sems,
    ) = refs[10:]
    loads = [
        pltpu.make_async_copy(source, target, load_sems.at[k])
        for k, (source, target) in enumerate(zip(operands, refs[10:16]))
    ]
    for k in (0, 2, 5, 1, 3, 4):
        loads[k].start()
    x_gco, x_gfi = x_ctx, x_feat
    rows, cols, chans, scale, n_row, n_col, orders = dims
    mix = s_pair.at[0, pl.ds(0, chans // LANES)]
    h, w = rows // 2, cols // 2
    cells = h * w
    r = lax.axis_index("row")
    c = lax.axis_index("col")
    has_up, has_down = r > 0, r < n_row - 1
    has_left, has_right = c > 0, c < n_col - 1
    vertical = {-1: has_up, 0: None, 1: has_down}
    horizontal = {-1: has_left, 0: None, 1: has_right}

    def neighbour(d):
        down, right = DIRECTIONS[d]
        device = {}
        if down:
            device["row"] = r + down
        if right:
            device["col"] = c + right
        if not right:
            return vertical[down], device
        if not down:
            return horizontal[right], device
        return jnp.logical_and(vertical[down], horizontal[right]), device

    sides = [neighbour(d) for d in range(8)]

    halos[...] = jnp.zeros_like(halos)
    barrier = pltpu.get_barrier_semaphore()
    for has, device in sides:
        @pl.when(has)
        def _(device=device):
            pl.semaphore_signal(
                barrier, inc=1, device_id=device, device_id_type=pl.DeviceIdType.MESH
            )
    count = n_row * n_col
    bits = count.bit_length() - 1
    col_bits = n_col.bit_length() - 1
    me = r * n_col + c

    def bit_of(b):
        return me // 2**b % 2

    def reach(group, mask):
        row, col = r, c
        for q, b in enumerate(group):
            if mask >> q & 1:
                if b < col_bits:
                    col = col + 2**b * (1 - 2 * bit_of(b))
                else:
                    row = row + 2 ** (b - col_bits) * (1 - 2 * bit_of(b))
        return {"row": row, "col": col}

    partners = {}
    for order in orders:
        for group in order:
            for mask in range(1, 2 ** len(group)):
                flips = tuple(b for q, b in enumerate(group) if mask >> q & 1)
                partners[flips] = reach(group, mask)
    for device in partners.values():
        pl.semaphore_signal(
            barrier, inc=1, device_id=device, device_id_type=pl.DeviceIdType.MESH
        )

    for ref in (s_fine, s_pool, s_noise, s_ctx, s_corner, fine):
        ref[...] = jnp.zeros_like(ref)

    def enter():
        pl.semaphore_wait(barrier, len(partners) + sum(has.astype(jnp.int32) for has, _device in sides))

    def each(n, body):
        if n <= 16:
            for j in range(n):
                body(j)
        else:
            pl.loop(0, n)(body)

    def chain(number, order, out, out_at):
        acc, send, recv = sums[number], outgoing[number], incoming[number]
        state = {"step": 0, "copies": []}
        frees = [[b for b in range(bits) if b not in sum(order[:k], ())] for k in range(len(order) + 1)]
        lefts = [2 ** len(free) for free in frees]
        bases = [count - left for left in lefts]

        def arrived(k, slot):
            total = None
            for mask in range(1, 2 ** len(order[k])):
                part = recv[bases[k] + (mask - 1) * lefts[k + 1] + slot].astype(F32)
                total = part if total is None else total + part
            return total

        def begin(half):
            n = lefts[1] // 2
            at = half * n
            other = 1 - bit_of(order[0][0])

            def fill(j):
                send[at + j] = acc[2 * (at + j) + other].astype(BF16)

            each(n, fill)
            copy = pltpu.make_async_remote_copy(
                src_ref=send.at[pl.ds(at, n)],
                dst_ref=recv.at[pl.ds(at, n)],
                send_sem=chain_sems.at[number, 0, half, 0],
                recv_sem=chain_sems.at[number, 0, half, 1],
                device_id=reach(order[0], 1),
                device_id_type=pl.DeviceIdType.MESH,
            )
            copy.start()
            state["copies"].append(copy)
            state["step"] = 1

        def step():
            k = state["step"]
            if k > len(order):
                return
            state["step"] = k + 1
            for copy in state["copies"]:
                copy.wait()
            state["copies"] = []
            if k == len(order):
                total = scale * (acc[me] + arrived(k - 1, 0))
                per = total.shape[0]
                stride = out.shape[0] // per
                for d in range(total.shape[1] // LANES):
                    out[pl.ds(out_at // LANES + d, per, stride=stride), :] = total[
                        :, d * LANES : (d + 1) * LANES
                    ]
                return
            group, free, n = order[k], frees[k], lefts[k + 1]
            rest = frees[k + 1]
            fixed = sum((bit_of(b) * 2**b for b in range(bits) if b not in free), 0)

            def value(j, mask):
                index, slot = fixed, 0
                for q, b in enumerate(free):
                    if b in group:
                        flip = mask >> group.index(b) & 1
                        bit = 1 - bit_of(b) if flip else bit_of(b)
                    else:
                        bit = j // 2 ** rest.index(b) % 2
                    index = index + bit * 2**b
                    slot = slot + bit * 2**q
                total = acc[index]
                if k > 0:
                    total = total + arrived(k - 1, slot)
                return index, total

            for mask in reversed(range(1, 2 ** len(group))):
                at = (mask - 1) * n

                def fill(j, mask=mask, at=at):
                    send[at + j] = value(j, mask)[1].astype(BF16)

                each(n, fill)
                copy = pltpu.make_async_remote_copy(
                    src_ref=send.at[pl.ds(at, n)],
                    dst_ref=recv.at[pl.ds(bases[k] + at, n)],
                    send_sem=chain_sems.at[number, k, mask - 1, 0],
                    recv_sem=chain_sems.at[number, k, mask - 1, 1],
                    device_id=reach(group, mask),
                    device_id_type=pl.DeviceIdType.MESH,
                )
                copy.start()
                state["copies"].append(copy)

            def keep(j):
                index, total = value(j, 0)
                acc[index] = total

            if k > 0:
                each(n, keep)

        return step, begin


    pieces = chans // LANES
    post_chains = [chain(k, orders[k], out_post, k * LANES) for k in range(pieces)]
    middle_chains = [chain(k, orders[k], out_coarse, (k - pieces) * LANES) for k in range(pieces, 2 * pieces)]
    prior_chains = [
        chain(k, orders[k], out_prior, (k - 2 * pieces) * LANES)
        for k in range(2 * pieces, 4 * pieces)
    ]

    early, late = prior_chains[:2], prior_chains[2:]

    def advance(chains):
        for step, _begin in chains:
            step()

    def begin(chains, tap):
        if tap in (4, 8):
            for _step, start_half in chains:
                start_half(tap // 8)

    parts_post = [(sums[k], k * LANES) for k in range(pieces)]
    parts_coarse = [(sums[k + pieces], k * LANES) for k in range(pieces)]
    parts_prior = [(sums[2 * pieces + k], k % pieces * LANES) for k in range(2 * pieces)]

    def spread(parts, start, values):
        height = values.shape[0]
        for acc, at in parts:
            per, width = acc.shape[1:]
            row = start
            while row < start + height:
                inner = row % per
                size = min(per - inner, start + height - row)
                acc[row // per, inner : inner + size] = values[
                    row - start : row - start + size, at : at + width
                ]
                row += size


    def copies(index, sizes):
        found = []
        for d in range(8):
            size = sizes[0] if d < 4 else sizes[1]
            found.append(
                pltpu.make_async_remote_copy(
                    src_ref=edges.at[index, d, pl.ds(0, size)],
                    dst_ref=halos.at[index, OPPOSITE[d], pl.ds(0, size)],
                    send_sem=sems.at[index, d],
                    recv_sem=sems.at[index, 8 + OPPOSITE[d]],
                    device_id=sides[d][1],
                    device_id_type=pl.DeviceIdType.MESH,
                )
            )
        return found

    def start(index, sizes, parts):
        found = copies(index, sizes)
        for d in (4, 5, 6, 7, 0, 1, 2, 3):
            at = 0
            for part in parts[d]:
                edges[index, d, at : at + part.shape[0], :] = part.astype(BF16)
                at += part.shape[0]
            pl.when(sides[d][0])(found[d].start)
        return found

    def finish(found):
        for d in range(8):
            @pl.when(sides[d][0])
            def _(d=d):
                found[d].wait_send()
                found[OPPOSITE[d]].wait_recv()

    def halo(index, d, at, size):
        return halos[index, d, at : at + size, :].astype(F32)

    def corner(k, *pieces):
        at = k * CORNER
        for piece in pieces:
            put(s_corner, pl.ds(at, piece.shape[0]), piece)
            at += piece.shape[0]
        return (get(s_corner, pl.ds(k * CORNER, CORNER)),)

    def view(x, t, u):
        return x[t % 2, u + 1, pl.ds(w if t >= 1 else 0, cells), :]

    def dot_in(x, g):
        return lax.dot_general(x, g, (((0,), (0,)), ((), ())), preferred_element_type=F32)

    def dot_out(g, weights):
        return lax.dot_general(g, weights, (((1,), (1,)), ((), ())), preferred_element_type=F32)

    def tap_of(weights, a, b):
        k = weights.shape[0] // 9
        return weights[(3 * a + b) * k : (3 * a + b + 1) * k, :]

    fine_stride = cols + 2 * EDGE
    stride = w + 2 * EDGE
    extra = round_up(h + 1, 16)
    side = round_up(h + 2, 8)
    phases = [(p, q) for p in range(2) for q in range(2)]

    loads[0].wait()
    loads[2].wait()
    for i in range(rows):
        put(
            s_fine,
            pl.ds((i + 1) * fine_stride + EDGE, cols),
            feat[pl.ds(i * cols, cols), :].astype(F32),
        )
    for i in range(h):
        put(s_noise, pl.ds((i + 1) * stride + EDGE, w), noise_coarse[pl.ds(i * w, w), :])
    top, bottom = feat[0:cols, :], feat[(rows - 1) * cols :, :]
    noise_top, noise_bottom = noise_coarse[0:w, :], noise_coarse[(h - 1) * w :, :]
    parts = [
        (top, noise_top),
        (bottom, noise_bottom),
        (
            get(s_fine, pl.ds(fine_stride + EDGE, rows, stride=fine_stride)),
            get(s_noise, pl.ds(stride + EDGE, h, stride=stride)),
        ),
        (
            get(s_fine, pl.ds(fine_stride + EDGE + cols - 1, rows, stride=fine_stride)),
            get(s_noise, pl.ds(stride + EDGE + w - 1, h, stride=stride)),
        ),
    ]
    for k in range(4):
        i, j = k // 2, k % 2
        at = (i * (rows - 1) + 1) * fine_stride + EDGE + j * (cols - 1)
        noise_at = (i * (h - 1) + 1) * stride + EDGE + j * (w - 1)
        parts.append(corner(k, get(s_fine, pl.ds(at, 1)), get(s_noise, pl.ds(noise_at, 1))))
    enter()
    found = start(0, (cols + w, CORNER), parts)

    loads[5].wait()
    for p, q in phases:
        for kr in range(2):
            for kc in range(2):
                total = None
                for a in TAPS[p][kr]:
                    for b in TAPS[q][kc]:
                        part = tap_of(w_prior, a, b).astype(F32)
                        total = part if total is None else total + part
                w_sums[((2 * p + kr) * 2 + q) * 2 + kc] = total.astype(BF16)

    def own(p):
        return slice(p * w, p * w + cells)

    loads[1].wait()
    put(mix, pl.ds(0, rows * cols), noise_fine[...])
    for p, q in phases:
        for i in range(h):
            fine[2 * p + q, (i + p) * w : (i + p + 1) * w, :] = get(
                mix, pl.ds((2 * i + p) * cols + q, w, stride=2)
            )

    def fill_feat(i, ms):
        p = i % 2
        at = (i - p) // 2 + p
        for m in ms:
            x_feat[p, m, at * w : (at + 1) * w, :] = get(
                s_fine, pl.ds((i + 1) * fine_stride + EDGE - 1 + m, w, stride=2)
            ).astype(BF16)

    for i in range(rows):
        fill_feat(i, (1, 2))
    def dot_fine(p, q, a, b):
        x = view(x_feat, p + a - 1, q + b - 1)
        return jnp.dot(x, tap_of(w_post, a, b), preferred_element_type=F32)

    loads[3].wait()
    for p, q in phases:
        total = None
        for a in range(1 - p, 3 - p):
            for b in range(1 - q, 3 - q):
                part = dot_fine(p, q, a, b)
                total = part if total is None else total + part
        fine[2 * p + q, own(p), :] = total + fine[2 * p + q, own(p), :]
    finish(found)
    put(s_fine, pl.ds(EDGE, cols), halo(0, UP, 0, cols))
    put(s_fine, pl.ds((rows + 1) * fine_stride + EDGE, cols), halo(0, DOWN, 0, cols))
    put(s_fine, pl.ds(fine_stride + EDGE - 1, rows, stride=fine_stride), halo(0, LEFT, 0, rows))
    put(s_fine, pl.ds(fine_stride + EDGE + cols, rows, stride=fine_stride), halo(0, RIGHT, 0, rows))
    put(s_fine, pl.ds(EDGE - 1, 1), halo(0, UP_LEFT, 0, CORNER)[0:1])
    put(s_fine, pl.ds(EDGE + cols, 1), halo(0, UP_RIGHT, 0, CORNER)[0:1])
    last = (rows + 1) * fine_stride + EDGE
    put(s_fine, pl.ds(last - 1, 1), halo(0, DOWN_LEFT, 0, CORNER)[0:1])
    put(s_fine, pl.ds(last + cols, 1), halo(0, DOWN_RIGHT, 0, CORNER)[0:1])
    for i in range(rows):
        fill_feat(i, (0, 3))
    fill_feat(-1, (0, 1, 2, 3))
    fill_feat(rows, (0, 1, 2, 3))

    pooled = None
    for p, q in phases:
        total = None
        for a in range(3):
            for b in range(3):
                if p + a - 1 in (0, 1) and q + b - 1 in (0, 1):
                    continue
                part = dot_fine(p, q, a, b)
                total = part if total is None else total + part
        total = total + fine[2 * p + q, own(p), :]
        fine[2 * p + q, own(p), :] = total
        pooled = total if pooled is None else pooled + total
    pooled = (0.25 * pooled).astype(BF16).astype(F32)
    for i in range(h):
        put(s_pool, pl.ds((i + 2) * stride + EDGE, w), pooled[i * w : (i + 1) * w])

    def line(p, q, i):
        return fine[2 * p + q, (i + p) * w : (i + p + 1) * w, :]

    def column(values, j):
        put(mix, pl.ds(0, cells), values)
        return get(mix, pl.ds(j, h, stride=w))

    pool_top, pool_bottom = pooled[0 : 2 * w], pooled[(h - 2) * w :]

    def pool_column(j):
        return get(s_pool, pl.ds(2 * stride + EDGE + j, h, stride=stride))

    lefts = [column(fine[2 * p, own(p), :], 0) for p in range(2)]
    rights = [column(fine[2 * p + 1, own(p), :], w - 1) for p in range(2)]
    parts = [
        (pool_top, line(0, 0, 0), line(0, 1, 0)),
        (pool_bottom, line(1, 0, h - 1), line(1, 1, h - 1)),
        (pool_column(0), pool_column(1), *lefts),
        (pool_column(w - 2), pool_column(w - 1), *rights),
    ]
    for k in range(4):
        i, j = k // 2, k % 2
        at = (i * (h - 2) + 2) * stride + EDGE + j * (w - 2)
        cell = line(i, j, i * (h - 1))[j * (w - 1) : j * (w - 1) + 1]
        parts.append(
            corner(k, get(s_pool, pl.ds(at, 2)), get(s_pool, pl.ds(at + stride, 2)), cell)
        )
    found = start(1, (4 * w, CORNER), parts)
    for i in range(h):
        put(s_noise, pl.ds((i + 1) * stride + EDGE, w), noise_coarse[pl.ds(i * w, w), :])
    put(s_noise, pl.ds(EDGE, w), halo(0, UP, cols, w))
    put(s_noise, pl.ds((h + 1) * stride + EDGE, w), halo(0, DOWN, cols, w))
    put(s_noise, pl.ds(stride + EDGE - 1, h, stride=stride), halo(0, LEFT, rows, h))
    put(s_noise, pl.ds(stride + EDGE + w, h, stride=stride), halo(0, RIGHT, rows, h))
    put(s_noise, pl.ds(EDGE - 1, 1), halo(0, UP_LEFT, 0, CORNER)[1:2])
    put(s_noise, pl.ds(EDGE + w, 1), halo(0, UP_RIGHT, 0, CORNER)[1:2])
    last = (h + 1) * stride + EDGE
    put(s_noise, pl.ds(last - 1, 1), halo(0, DOWN_LEFT, 0, CORNER)[1:2])
    put(s_noise, pl.ds(last + w, 1), halo(0, DOWN_RIGHT, 0, CORNER)[1:2])
    finish(found)
    for k in range(2):
        put(s_pool, pl.ds(k * stride + EDGE, w), halo(1, UP, k * w, w))
        put(s_pool, pl.ds((h + 2 + k) * stride + EDGE, w), halo(1, DOWN, k * w, w))
        put(s_pool, pl.ds(2 * stride + EDGE - 2 + k, h, stride=stride), halo(1, LEFT, k * h, h))
        put(s_pool, pl.ds(2 * stride + EDGE + w + k, h, stride=stride), halo(1, RIGHT, k * h, h))
        put(s_pool, pl.ds(k * stride + EDGE - 2, 2), halo(1, UP_LEFT, 0, CORNER)[2 * k : 2 * k + 2])
        put(s_pool, pl.ds(k * stride + EDGE + w, 2), halo(1, UP_RIGHT, 0, CORNER)[2 * k : 2 * k + 2])
        at = (h + 2 + k) * stride + EDGE
        put(s_pool, pl.ds(at - 2, 2), halo(1, DOWN_LEFT, 0, CORNER)[2 * k : 2 * k + 2])
        put(s_pool, pl.ds(at + w, 2), halo(1, DOWN_RIGHT, 0, CORNER)[2 * k : 2 * k + 2])
    base = cells + w
    for q in range(2):
        fine[q, cells : cells + w, :] = halo(1, DOWN, (2 + q) * w, w)
        fine[2 + q, 0:w, :] = halo(1, UP, (2 + q) * w, w)
    for p in range(2):
        fine[2 * p, base + p : base + p + h, :] = halo(1, RIGHT, (2 + p) * h, h)
        fine[2 * p + 1, base + p : base + p + h, :] = halo(1, LEFT, (2 + p) * h, h)
    fine[3, base : base + 1, :] = halo(1, UP_LEFT, 0, CORNER)[4:5]
    fine[2, base : base + 1, :] = halo(1, UP_RIGHT, 0, CORNER)[4:5]
    fine[1, base + h : base + h + 1, :] = halo(1, DOWN_LEFT, 0, CORNER)[4:5]
    fine[0, base + h : base + h + 1, :] = halo(1, DOWN_RIGHT, 0, CORNER)[4:5]

    loads[4].wait()
    for i in range(h + 4):
        for b in range(3):
            x_pool[b, i * w : (i + 1) * w, :] = get(
                s_pool, pl.ds(i * stride + EDGE + b - 1, w)
            ).astype(BF16)
    for a in range(3):
        for b in range(3):
            both = [
                get(s_pool, pl.ds(a * stride + EDGE - 2 + b, side, stride=stride)),
                get(s_pool, pl.ds(a * stride + EDGE + w - 1 + b, side, stride=stride)),
            ]
            side_pool[3 * a + b] = jnp.concatenate(both, axis=0).astype(BF16)
    ring = (h + 2) * w
    noise = jnp.concatenate(
        [get(s_noise, pl.ds(i * stride + EDGE, w)) for i in range(h + 2)]
        + [
            get(s_noise, pl.ds(EDGE - 1, side, stride=stride)),
            get(s_noise, pl.ds(EDGE + w, side, stride=stride)),
        ],
        axis=0,
    )
    total = None
    for a in range(3):
        for b in range(3):
            x = jnp.concatenate([x_pool[b, pl.ds(a * w, ring), :], side_pool[3 * a + b]], axis=0)
            part = jnp.dot(x, tap_of(w_coarse, a, b), preferred_element_type=F32)
            total = part if total is None else total + part
    total = total + noise
    coarse[...] = total[w : w + cells]
    total = total.astype(BF16).astype(F32)
    put(s_ctx, pl.ds(EDGE, w), jnp.where(has_up, total[0:w], 0.0))
    for i in range(1, h + 1):
        put(s_ctx, pl.ds(i * stride + EDGE, w), total[i * w : (i + 1) * w])
    put(s_ctx, pl.ds((h + 1) * stride + EDGE, w), jnp.where(has_down, total[ring - w : ring], 0.0))
    place = lax.broadcasted_iota(jnp.int32, (side, chans), 0)
    first = jnp.where(has_up, 0, 1)
    limit = jnp.where(has_down, h + 2, h + 1)
    inside = jnp.logical_and(place >= first, place < limit)
    for at, has, values in (
        (EDGE - 1, has_left, total[ring : ring + side]),
        (EDGE + w, has_right, total[ring + side :]),
    ):
        put(
            s_ctx,
            pl.ds(at, side, stride=stride),
            jnp.where(jnp.logical_and(inside, has), values, 0.0),
        )
    for i in range(h + 2):
        for k in range(3):
            x_ctx[k, i * w : (i + 1) * w, :] = get(
                s_ctx, pl.ds(i * stride + EDGE + k - 1, w)
            ).astype(BF16)
    for q in range(2):
        for kr in range(2):
            for kc in range(2):
                at = kr * stride + EDGE + (w - 1 if q == 0 else -1) + kc
                side_ctx[(2 * q + kr) * 2 + kc] = get(
                    s_ctx, pl.ds(at, extra, stride=stride)
                ).astype(BF16)

    place = lax.broadcasted_iota(jnp.int32, (extra, 2 * chans), 0)
    for p, q in phases:
        prior = None
        for kr in range(2):
            for kc in range(2):
                x = jnp.concatenate(
                    [x_ctx[q + kc, pl.ds(kr * w, base), :], side_ctx[(2 * q + kr) * 2 + kc]],
                    axis=0,
                )
                part = jnp.dot(
                    x, w_sums[((2 * p + kr) * 2 + q) * 2 + kc], preferred_element_type=F32
                )
                prior = part if prior is None else prior + part
        raw = prior[:, chans:]
        small = jnp.exp(-jnp.abs(raw))
        sigma = jnp.maximum(raw, 0.0) + jnp.log1p(small) + 0.5
        whole = 1.0 + small
        both_inverse = 1.0 / (sigma * whole)
        gate = jnp.where(raw >= 0, 1.0, small) * (sigma * both_inverse)
        inverse = whole * both_inverse
        ratio = (fine[2 * p + q] - prior[:, :chans]) * inverse
        residual = ratio * inverse
        err[2 * p + q] = residual[own(p)]
        slope = (inverse - ratio * ratio * inverse) * gate
        both = jnp.concatenate([-residual, slope], axis=1).astype(BF16).astype(F32)
        if p == 0:
            g_main[q, 0:cells, :] = both[0:cells]
            g_main[q, cells:, :] = jnp.where(has_down, both[cells:base], 0.0)
            inside = jnp.logical_or(has_down, place < h)
        else:
            g_main[2 + q, 0:w, :] = jnp.where(has_up, both[0:w], 0.0)
            g_main[2 + q, w:, :] = both[w:base]
            inside = jnp.logical_or(has_up, place > 0)
        inside = jnp.logical_and(inside, has_left if q else has_right)
        g_side[2 * p + q] = jnp.where(inside, both[base:], 0.0)

    windows = ((1, 1), (0, 1), (0, 0))
    for a in range(3):
        i0, i1 = windows[a]
        for q in range(2):
            total = g_main[q, pl.ds(i0 * w, cells), :] + g_main[2 + q, pl.ds(i1 * w, cells), :]
            for i in range(h):
                put(s_pair.at[q], pl.ds(i * stride + EDGE, w), total[i * w : (i + 1) * w])
            total = g_side[q, i0 : i0 + h, :] + g_side[2 + q, i1 : i1 + h, :]
            put(s_pair.at[q], pl.ds(EDGE - 1 if q else EDGE + w, h, stride=stride), total)
        for i in range(h):
            at = i * stride + EDGE
            even, odd = get(s_pair.at[0], pl.ds(at, w)), get(s_pair.at[1], pl.ds(at, w))
            here = slice(i * w, (i + 1) * w)
            boxes[3 * a, here, :] = (odd + get(s_pair.at[0], pl.ds(at + 1, w))).astype(BF16)
            boxes[3 * a + 1, here, :] = (even + odd).astype(BF16)
            boxes[3 * a + 2, here, :] = (get(s_pair.at[1], pl.ds(at - 1, w)) + even).astype(BF16)

    total = None
    for tap in range(9):
        part = dot_out(boxes[tap], tap_of(w_prior, tap // 3, tap % 3))
        total = part if total is None else total + part
    total = (coarse[...] + total).astype(BF16).astype(F32)

    def pad_lines(values):
        for i in range(h):
            put(s_pool, pl.ds((i + 1) * stride + EDGE, w), values[i * w : (i + 1) * w])

    pad_lines(total)
    parts = [
        (total[0:w],),
        (total[cells - w :],),
        (get(s_pool, pl.ds(stride + EDGE, h, stride=stride)),),
        (get(s_pool, pl.ds(stride + EDGE + w - 1, h, stride=stride)),),
    ]
    for k in range(4):
        i, j = k // 2, k % 2
        at = (i * (h - 1) + 1) * stride + EDGE + j * (w - 1)
        parts.append(corner(k, get(s_pool, pl.ds(at, 1))))
    found = start(2, (w, CORNER), parts)
    for part in range(2):
        for tap in range(9):
            spread(
                parts_prior[2 * part : 2 * part + 2],
                tap * chans,
                dot_in(
                    x_ctx[1, pl.ds(w, cells), :], boxes[tap, :, part * chans : (part + 1) * chans]
                ),
            )
            begin(prior_chains[2 * part : 2 * part + 2], tap)
    gco = total.astype(BF16)
    for a in range(3):
        for b in range(3):
            spread(
                parts_coarse,
                (3 * a + b) * chans,
                dot_in(x_pool[b, pl.ds((a + 1) * w, cells), :], gco),
            )
            begin(middle_chains, 3 * a + b)
    advance(early)
    advance(late)
    advance(middle_chains)
    finish(found)

    put(s_pool, pl.ds(EDGE, w), halo(2, UP, 0, w))
    put(s_pool, pl.ds((h + 1) * stride + EDGE, w), halo(2, DOWN, 0, w))
    put(s_pool, pl.ds(stride + EDGE - 1, h, stride=stride), halo(2, LEFT, 0, h))
    put(s_pool, pl.ds(stride + EDGE + w, h, stride=stride), halo(2, RIGHT, 0, h))
    put(s_pool, pl.ds(EDGE - 1, 1), halo(2, UP_LEFT, 0, CORNER)[0:1])
    put(s_pool, pl.ds(EDGE + w, 1), halo(2, UP_RIGHT, 0, CORNER)[0:1])
    last = (h + 1) * stride + EDGE
    put(s_pool, pl.ds(last - 1, 1), halo(2, DOWN_LEFT, 0, CORNER)[0:1])
    put(s_pool, pl.ds(last + w, 1), halo(2, DOWN_RIGHT, 0, CORNER)[0:1])
    for i in range(h + 2):
        for k in range(3):
            x_gco[k, i * w : (i + 1) * w, :] = get(
                s_pool, pl.ds(i * stride + EDGE + k - 1, w)
            ).astype(BF16)
    total = None
    for a in range(3):
        for b in range(3):
            part = dot_out(x_gco[2 - b, pl.ds((2 - a) * w, cells), :], tap_of(w_coarse, a, b))
            total = part if total is None else total + part
    total = 0.25 * total

    for p, q in phases:
        own_gfi[2 * p + q] = (err[2 * p + q] + total).astype(BF16)

    def s_gfi(q):
        return s_pair.at[q, pl.ds(0, chans // LANES)]

    def gfi_line(p, q, i):
        return own_gfi[2 * p + q, i * w : (i + 1) * w, :]

    for p, q in phases:
        for i in range(h):
            put(
                s_gfi(q),
                pl.ds((i + p * h) * stride + EDGE, w),
                own_gfi[2 * p + q, i * w : (i + 1) * w, :].astype(F32),
            )

    def gfi_column(p, q):
        at = p * h * stride + EDGE + (w - 1 if q else 0)
        return get(s_gfi(q), pl.ds(at, h, stride=stride))

    parts = [
        (gfi_line(0, 0, 0), gfi_line(0, 1, 0)),
        (gfi_line(1, 0, h - 1), gfi_line(1, 1, h - 1)),
        (gfi_column(0, 0), gfi_column(1, 0)),
        (gfi_column(0, 1), gfi_column(1, 1)),
    ]
    for k in range(4):
        i, j = k // 2, k % 2
        at = i * (2 * h - 1) * stride + EDGE + j * (w - 1)
        parts.append(corner(k, get(s_gfi(j), pl.ds(at, 1))))
    found = start(3, (2 * w, CORNER), parts)
    for a in range(3):
        for b in range(3):
            total = None
            for p, q in phases:
                part = dot_in(view(x_feat, p + a - 1, q + b - 1), own_gfi[2 * p + q])
                total = part if total is None else total + part
            spread(parts_post, (3 * a + b) * chans, total)
            begin(post_chains, 3 * a + b)
    advance(post_chains)
    advance(prior_chains)
    advance(middle_chains)
    finish(found)
    for p in range(2):
        put(s_gfi(1), pl.ds(p * h * stride + EDGE - 1, h, stride=stride), halo(3, LEFT, p * h, h))
        put(s_gfi(0), pl.ds(p * h * stride + EDGE + w, h, stride=stride), halo(3, RIGHT, p * h, h))
        for q in range(2):
            x_gfi[p, 1 + q, p * w : p * w + cells, :] = own_gfi[2 * p + q]
            x_gfi[p, 1 + q, (1 - p) * cells : (1 - p) * cells + w, :] = halos[
                3, UP if p else DOWN, q * w : (q + 1) * w, :
            ]
        for i in range(h):
            here = slice((i + p) * w, (i + p + 1) * w)
            at = (i + p * h) * stride + EDGE
            x_gfi[p, 0, here, :] = get(s_gfi(1), pl.ds(at - 1, w)).astype(BF16)
            x_gfi[p, 3, here, :] = get(s_gfi(0), pl.ds(at + 1, w)).astype(BF16)
        ring_at = slice((1 - p) * cells, (1 - p) * cells + w)
        vertical_side = UP if p else DOWN
        left = halo(3, UP_LEFT if p else DOWN_LEFT, 0, CORNER)[0:1]
        right = halo(3, UP_RIGHT if p else DOWN_RIGHT, 0, CORNER)[0:1]
        put(s_gfi(1), pl.ds(EDGE - 1, 1), left)
        put(s_gfi(1), pl.ds(EDGE, w), halo(3, vertical_side, w, w))
        put(s_gfi(0), pl.ds(EDGE, w), halo(3, vertical_side, 0, w))
        put(s_gfi(0), pl.ds(EDGE + w, 1), right)
        x_gfi[p, 0, ring_at, :] = get(s_gfi(1), pl.ds(EDGE - 1, w)).astype(BF16)
        x_gfi[p, 3, ring_at, :] = get(s_gfi(0), pl.ds(EDGE + 1, w)).astype(BF16)
    for p, q in phases:
        total = None
        for a in range(3):
            for b in range(3):
                part = dot_out(view(x_gfi, p - a + 1, q - b + 1), tap_of(w_post, a, b))
                total = part if total is None else total + part
        for i in range(h):
            put(mix, pl.ds((2 * i + p) * cols + q, w, stride=2), total[i * w : (i + 1) * w])
    grad_feat[...] = get(mix, pl.ds(0, rows * cols)).astype(BF16)
    advance(post_chains)
    advance(prior_chains)
    advance(middle_chains)
    advance(post_chains)
    advance(prior_chains)
    advance(middle_chains)
    for _ in range(bits):
        advance(prior_chains + middle_chains + post_chains)


def hand_out(*refs):
    for source, target in zip(refs[:4], refs[4:]):
        target[...] = source[...]


def orders_of(n_row, n_col, pieces):
    bits = (n_row * n_col).bit_length() - 1
    near, a, b = (0,), 1, n_col.bit_length() - 1
    far = [k for k in range(1, bits) if k not in (a, b)]
    pairs = [tuple(far[k : k + 2]) for k in range(0, len(far), 2)]
    singles = [(k,) for k in far]
    post = (near, (a, b), *pairs)
    middle = (near, singles[0], (a, b), *singles[1:])
    prior = ((near, (b,), (a,), *pairs), (near, (a,), (b,), *pairs))
    mixed = ((post, middle)[k % 2] for k in range(pieces))
    return (*mixed, *(middle,) * pieces, *prior * pieces)


def on_device(sizes, feat, noise_fine, noise_coarse, w_post, w_coarse, w_prior):
    n_row, n_col = sizes
    rows, cols, chans = feat.shape
    h, w = rows // 2, cols // 2
    scale = 1.0 / math.sqrt(rows * n_row * cols * n_col)
    cells, quarter = rows * cols, h * w
    vmem = pl.BlockSpec(memory_space=pltpu.VMEM)
    count = n_row * n_col
    orders = orders_of(n_row, n_col, chans // LANES)
    dims = (rows, cols, chans, scale, n_row, n_col, orders)
    per = w_post.shape[0] // count
    widths = (LANES,) * len(orders)
    anywhere = pl.BlockSpec(memory_space=pl.ANY)
    extra, side, stride = round_up(h + 1, 16), round_up(h + 2, 8), w + 2 * EDGE

    def lanes(n, depth=chans):
        return pltpu.VMEM((depth // LANES, n, LANES), F32)

    grad_feat, out_post, out_coarse, out_prior = pl.pallas_call(
        functools.partial(tile_kernel, dims),
        out_shape=(
            pltpu.VMEM((cells, chans), BF16),
            pltpu.VMEM((per * chans // LANES, LANES), F32),
            pltpu.VMEM((per * chans // LANES, LANES), F32),
            pltpu.VMEM((per * 2 * chans // LANES, LANES), F32),
        ),
        in_specs=[anywhere] * 6,
        out_specs=(vmem,) * 4,
        scratch_shapes=[
            pltpu.VMEM((cells, chans), BF16),
            pltpu.VMEM((cells, chans), F32),
            pltpu.VMEM((quarter, chans), F32),
            pltpu.VMEM(w_post.shape, BF16),
            pltpu.VMEM(w_coarse.shape, BF16),
            pltpu.VMEM(w_prior.shape, BF16),
            pltpu.VMEM((4, (h + 1) * w + extra, chans), F32),
            pltpu.VMEM((4, quarter, chans), F32),
            pltpu.VMEM((quarter, chans), F32),
            lanes((rows + 2) * (cols + 2 * EDGE)),
            lanes((side + 2) * stride),
            lanes(side * stride),
            lanes((extra + 1) * stride),
            pltpu.VMEM((2, 2 * chans // LANES, max(2 * h * stride, cells), LANES), F32),
            lanes(4 * CORNER),
            pltpu.VMEM((2, 4, (h + 1) * w, chans), BF16),
            pltpu.VMEM((3, (h + 4) * w, chans), BF16),
            pltpu.VMEM((9, 2 * side, chans), BF16),
            pltpu.VMEM((3, (h + 2) * w, chans), BF16),
            pltpu.VMEM((8, extra, chans), BF16),
            pltpu.VMEM((16, chans, 2 * chans), BF16),
            pltpu.VMEM((4, (h + 1) * w, 2 * chans), F32),
            pltpu.VMEM((4, extra, 2 * chans), F32),
            pltpu.VMEM((9, quarter, 2 * chans), BF16),
            pltpu.VMEM((4, quarter, chans), BF16),
            pltpu.VMEM((4, 8, 4 * w, chans), BF16),
            pltpu.VMEM((4, 8, 4 * w, chans), BF16),
            [pltpu.VMEM((count, per, width), F32) for width in widths],
            [pltpu.VMEM((count // 2, per, width), BF16) for width in widths],
            [pltpu.VMEM((count - 1, per, width), BF16) for width in widths],
            pltpu.SemaphoreType.DMA((4, 16)),
            pltpu.SemaphoreType.DMA((len(orders), max(map(len, orders)), 3, 2)),
            pltpu.SemaphoreType.DMA((6,)),
        ],
        compiler_params=pltpu.CompilerParams(
            collective_id=0, has_side_effects=True, vmem_limit_bytes=62 * 2**20
        ),
    )(
        feat.reshape(cells, chans),
        noise_fine.reshape(cells, chans),
        noise_coarse.reshape(quarter, chans),
        w_post,
        w_coarse,
        w_prior,
    )
    results = tuple(
        pltpu.with_memory_space_constraint(a, pltpu.VMEM)
        for a in (grad_feat, out_post, out_coarse, out_prior)
    )
    grad_feat, out_post, out_coarse, out_prior = pl.pallas_call(
        hand_out,
        out_shape=tuple(jax.ShapeDtypeStruct(a.shape, a.dtype) for a in results),
        in_specs=[vmem] * 4,
        out_specs=(vmem,) * 4,
    )(*results)
    return (
        grad_feat.reshape(rows, cols, chans),
        out_post.reshape(-1),
        out_coarse.reshape(-1),
        out_prior.reshape(-1),
    )


def solution(mesh):
    sizes = (mesh.shape["row"], mesh.shape["col"])
    return jax.shard_map(
        functools.partial(on_device, sizes),
        mesh=mesh,
        in_specs=(
            P("row", "col", None),
            P("row", "col", None),
            P("row", "col", None),
            P(),
            P(),
            P(),
        ),
        out_specs=(P("row", "col", None), P(("row", "col")), P(("row", "col")), P(("row", "col"))),
        check_vma=False,
    )
```

```python
import functools
import math

import jax
import jax.numpy as jnp
from jax import lax
from jax.experimental import pallas as pl
from jax.experimental.pallas import tpu as pltpu
from jax.sharding import PartitionSpec as P

F32 = jnp.float32
BF16 = jnp.bfloat16
EDGE = 8


LANES = 128


def put(ref, at, values):
    for d in range(values.shape[1] // LANES):
        ref[d, at, :] = values[:, d * LANES : (d + 1) * LANES]


def get(ref, at):
    return jnp.concatenate([ref[d, at, :] for d in range(ref.shape[0])], axis=1)


DIRECTIONS = ((-1, 0), (1, 0), (0, -1), (0, 1), (-1, -1), (-1, 1), (1, -1), (1, 1))
OPPOSITE = (1, 0, 3, 2, 7, 6, 5, 4)
UP, DOWN, LEFT, RIGHT, UP_LEFT, UP_RIGHT, DOWN_LEFT, DOWN_RIGHT = range(8)
CORNER = 16
TAPS = (((0,), (1, 2)), ((0, 1), (2,)))


def round_up(n, m):
    return -(-n // m) * m


def tile_kernel(
    dims,
    *refs,
):
    operands = refs[:6]
    grad_feat, out_post, out_coarse, out_prior = refs[6:10]
    (
        feat,
        noise_fine,
        noise_coarse,
        w_post,
        w_coarse,
        w_prior,
        fine,
        err,
        coarse,
        s_fine,
        s_pool,
        s_noise,
        s_ctx,
        s_pair,
        s_corner,
        x_feat,
        x_pool,
        side_pool,
        x_ctx,
        side_ctx,
        w_sums,
        g_main,
        g_side,
        boxes,
        own_gfi,
        edges,
        halos,
        sums,
        outgoing,
        incoming,
        sems,
        chain_sems,
        load_sems,
    ) = refs[10:]
    loads = [
        pltpu.make_async_copy(source, target, load_sems.at[k])
        for k, (source, target) in enumerate(zip(operands, refs[10:16]))
    ]
    for k in (0, 2, 5, 1, 3, 4):
        loads[k].start()
    x_gco, x_gfi = x_ctx, x_feat
    rows, cols, chans, scale, n_row, n_col, orders = dims
    mix = s_pair.at[0, pl.ds(0, chans // LANES)]
    h, w = rows // 2, cols // 2
    cells = h * w
    r = lax.axis_index("row")
    c = lax.axis_index("col")
    has_up, has_down = r > 0, r < n_row - 1
    has_left, has_right = c > 0, c < n_col - 1
    vertical = {-1: has_up, 0: None, 1: has_down}
    horizontal = {-1: has_left, 0: None, 1: has_right}

    def neighbour(d):
        down, right = DIRECTIONS[d]
        device = {}
        if down:
            device["row"] = r + down
        if right:
            device["col"] = c + right
        if not right:
            return vertical[down], device
        if not down:
            return horizontal[right], device
        return jnp.logical_and(vertical[down], horizontal[right]), device

    sides = [neighbour(d) for d in range(8)]

    halos[...] = jnp.zeros_like(halos)
    barrier = pltpu.get_barrier_semaphore()
    for has, device in sides:
        @pl.when(has)
        def _(device=device):
            pl.semaphore_signal(
                barrier, inc=1, device_id=device, device_id_type=pl.DeviceIdType.MESH
            )
    count = n_row * n_col
    bits = count.bit_length() - 1
    col_bits = n_col.bit_length() - 1
    me = r * n_col + c

    def bit_of(b):
        return me // 2**b % 2

    def reach(group, mask):
        row, col = r, c
        for q, b in enumerate(group):
            if mask >> q & 1:
                if b < col_bits:
                    col = col + 2**b * (1 - 2 * bit_of(b))
                else:
                    row = row + 2 ** (b - col_bits) * (1 - 2 * bit_of(b))
        return {"row": row, "col": col}

    partners = {}
    for order in orders:
        for group in order:
            for mask in range(1, 2 ** len(group)):
                flips = tuple(b for q, b in enumerate(group) if mask >> q & 1)
                partners[flips] = reach(group, mask)
    for device in partners.values():
        pl.semaphore_signal(
            barrier, inc=1, device_id=device, device_id_type=pl.DeviceIdType.MESH
        )

    for ref in (s_fine, s_pool, s_noise, s_ctx, s_corner, fine):
        ref[...] = jnp.zeros_like(ref)

    def enter():
        pl.semaphore_wait(barrier, len(partners) + sum(has.astype(jnp.int32) for has, _device in sides))

    def each(n, body):
        if n <= 16:
            for j in range(n):
                body(j)
        else:
            pl.loop(0, n)(body)

    def chain(number, order, out, out_at):
        acc, send, recv = sums[number], outgoing[number], incoming[number]
        state = {"step": 0, "copies": []}
        frees = [[b for b in range(bits) if b not in sum(order[:k], ())] for k in range(len(order) + 1)]
        lefts = [2 ** len(free) for free in frees]
        bases = [count - left for left in lefts]

        def arrived(k, slot):
            total = None
            for mask in range(1, 2 ** len(order[k])):
                part = recv[bases[k] + (mask - 1) * lefts[k + 1] + slot].astype(F32)
                total = part if total is None else total + part
            return total

        def begin(half):
            n = lefts[1] // 2
            at = half * n
            other = 1 - bit_of(order[0][0])

            def fill(j):
                send[at + j] = acc[2 * (at + j) + other].astype(BF16)

            each(n, fill)
            copy = pltpu.make_async_remote_copy(
                src_ref=send.at[pl.ds(at, n)],
                dst_ref=recv.at[pl.ds(at, n)],
                send_sem=chain_sems.at[number, 0, half, 0],
                recv_sem=chain_sems.at[number, 0, half, 1],
                device_id=reach(order[0], 1),
                device_id_type=pl.DeviceIdType.MESH,
            )
            copy.start()
            state["copies"].append(copy)
            state["step"] = 1

        def step():
            k = state["step"]
            if k > len(order):
                return
            state["step"] = k + 1
            for copy in state["copies"]:
                copy.wait()
            state["copies"] = []
            if k == len(order):
                total = scale * (acc[me] + arrived(k - 1, 0))
                per = total.shape[0]
                stride = out.shape[0] // per
                for d in range(total.shape[1] // LANES):
                    out[pl.ds(out_at // LANES + d, per, stride=stride), :] = total[
                        :, d * LANES : (d + 1) * LANES
                    ]
                return
            group, free, n = order[k], frees[k], lefts[k + 1]
            rest = frees[k + 1]
            fixed = sum((bit_of(b) * 2**b for b in range(bits) if b not in free), 0)

            def value(j, mask):
                index, slot = fixed, 0
                for q, b in enumerate(free):
                    if b in group:
                        flip = mask >> group.index(b) & 1
                        bit = 1 - bit_of(b) if flip else bit_of(b)
                    else:
                        bit = j // 2 ** rest.index(b) % 2
                    index = index + bit * 2**b
                    slot = slot + bit * 2**q
                total = acc[index]
                if k > 0:
                    total = total + arrived(k - 1, slot)
                return index, total

            for mask in reversed(range(1, 2 ** len(group))):
                at = (mask - 1) * n

                def fill(j, mask=mask, at=at):
                    send[at + j] = value(j, mask)[1].astype(BF16)

                each(n, fill)
                copy = pltpu.make_async_remote_copy(
                    src_ref=send.at[pl.ds(at, n)],
                    dst_ref=recv.at[pl.ds(bases[k] + at, n)],
                    send_sem=chain_sems.at[number, k, mask - 1, 0],
                    recv_sem=chain_sems.at[number, k, mask - 1, 1],
                    device_id=reach(group, mask),
                    device_id_type=pl.DeviceIdType.MESH,
                )
                copy.start()
                state["copies"].append(copy)

            def keep(j):
                index, total = value(j, 0)
                acc[index] = total

            if k > 0:
                each(n, keep)

        return step, begin


    pieces = chans // LANES
    post_chains = [chain(k, orders[k], out_post, k * LANES) for k in range(pieces)]
    middle_chains = [chain(k, orders[k], out_coarse, (k - pieces) * LANES) for k in range(pieces, 2 * pieces)]
    prior_chains = [
        chain(k, orders[k], out_prior, (k - 2 * pieces) * LANES)
        for k in range(2 * pieces, 4 * pieces)
    ]

    early, late = prior_chains[:2], prior_chains[2:]

    def advance(chains):
        for step, _begin in chains:
            step()

    def begin(chains, tap):
        if tap in (4, 8):
            for _step, start_half in chains:
                start_half(tap // 8)

    parts_post = [(sums[k], k * LANES) for k in range(pieces)]
    parts_coarse = [(sums[k + pieces], k * LANES) for k in range(pieces)]
    parts_prior = [(sums[2 * pieces + k], k % pieces * LANES) for k in range(2 * pieces)]

    def spread(parts, start, values):
        height = values.shape[0]
        for acc, at in parts:
            per, width = acc.shape[1:]
            row = start
            while row < start + height:
                inner = row % per
                size = min(per - inner, start + height - row)
                acc[row // per, inner : inner + size] = values[
                    row - start : row - start + size, at : at + width
                ]
                row += size


    def copies(index, sizes):
        found = []
        for d in range(8):
            size = sizes[0] if d < 4 else sizes[1]
            found.append(
                pltpu.make_async_remote_copy(
                    src_ref=edges.at[index, d, pl.ds(0, size)],
                    dst_ref=halos.at[index, OPPOSITE[d], pl.ds(0, size)],
                    send_sem=sems.at[index, d],
                    recv_sem=sems.at[index, 8 + OPPOSITE[d]],
                    device_id=sides[d][1],
                    device_id_type=pl.DeviceIdType.MESH,
                )
            )
        return found

    def start(index, sizes, parts):
        found = copies(index, sizes)
        for d in (0, 1, 4, 5, 6, 7, 2, 3):
            at = 0
            for part in parts[d]:
                edges[index, d, at : at + part.shape[0], :] = part.astype(BF16)
                at += part.shape[0]
            pl.when(sides[d][0])(found[d].start)
        return found

    def finish(found):
        for d in range(8):
            @pl.when(sides[d][0])
            def _(d=d):
                found[d].wait_send()
                found[OPPOSITE[d]].wait_recv()

    def halo(index, d, at, size):
        return halos[index, d, at : at + size, :].astype(F32)

    def corner(k, *pieces):
        at = k * CORNER
        for piece in pieces:
            put(s_corner, pl.ds(at, piece.shape[0]), piece)
            at += piece.shape[0]
        return (get(s_corner, pl.ds(k * CORNER, CORNER)),)

    def view(x, t, u):
        return x[t % 2, u + 1, pl.ds(w if t >= 1 else 0, cells), :]

    def dot_in(x, g):
        return lax.dot_general(x, g, (((0,), (0,)), ((), ())), preferred_element_type=F32)

    def dot_out(g, weights):
        return lax.dot_general(g, weights, (((1,), (1,)), ((), ())), preferred_element_type=F32)

    def tap_of(weights, a, b):
        k = weights.shape[0] // 9
        return weights[(3 * a + b) * k : (3 * a + b + 1) * k, :]

    fine_stride = cols + 2 * EDGE
    stride = w + 2 * EDGE
    extra = round_up(h + 1, 16)
    side = round_up(h + 2, 8)
    phases = [(p, q) for p in range(2) for q in range(2)]

    loads[0].wait()
    loads[2].wait()
    for i in range(rows):
        put(
            s_fine,
            pl.ds((i + 1) * fine_stride + EDGE, cols),
            feat[pl.ds(i * cols, cols), :].astype(F32),
        )
    for i in range(h):
        put(s_noise, pl.ds((i + 1) * stride + EDGE, w), noise_coarse[pl.ds(i * w, w), :])
    top, bottom = feat[0:cols, :], feat[(rows - 1) * cols :, :]
    noise_top, noise_bottom = noise_coarse[0:w, :], noise_coarse[(h - 1) * w :, :]
    parts = [
        (top, noise_top),
        (bottom, noise_bottom),
        (
            get(s_fine, pl.ds(fine_stride + EDGE, rows, stride=fine_stride)),
            get(s_noise, pl.ds(stride + EDGE, h, stride=stride)),
        ),
        (
            get(s_fine, pl.ds(fine_stride + EDGE + cols - 1, rows, stride=fine_stride)),
            get(s_noise, pl.ds(stride + EDGE + w - 1, h, stride=stride)),
        ),
    ]
    for k in range(4):
        i, j = k // 2, k % 2
        at = (i * (rows - 1) + 1) * fine_stride + EDGE + j * (cols - 1)
        noise_at = (i * (h - 1) + 1) * stride + EDGE + j * (w - 1)
        parts.append(corner(k, get(s_fine, pl.ds(at, 1)), get(s_noise, pl.ds(noise_at, 1))))
    enter()
    found = start(0, (cols + w, CORNER), parts)

    loads[5].wait()
    for p, q in phases:
        for kr in range(2):
            for kc in range(2):
                total = None
                for a in TAPS[p][kr]:
                    for b in TAPS[q][kc]:
                        part = tap_of(w_prior, a, b).astype(F32)
                        total = part if total is None else total + part
                w_sums[((2 * p + kr) * 2 + q) * 2 + kc] = total.astype(BF16)

    def own(p):
        return slice(p * w, p * w + cells)

    loads[1].wait()
    put(mix, pl.ds(0, rows * cols), noise_fine[...])
    for p, q in phases:
        for i in range(h):
            fine[2 * p + q, (i + p) * w : (i + p + 1) * w, :] = get(
                mix, pl.ds((2 * i + p) * cols + q, w, stride=2)
            )

    def fill_feat(i, ms):
        p = i % 2
        at = (i - p) // 2 + p
        for m in ms:
            x_feat[p, m, at * w : (at + 1) * w, :] = get(
                s_fine, pl.ds((i + 1) * fine_stride + EDGE - 1 + m, w, stride=2)
            ).astype(BF16)

    for i in range(rows):
        fill_feat(i, (1, 2))
    def dot_fine(p, q, a, b):
        x = view(x_feat, p + a - 1, q + b - 1)
        return jnp.dot(x, tap_of(w_post, a, b), preferred_element_type=F32)

    loads[3].wait()
    for p, q in phases:
        total = None
        for a in range(1 - p, 3 - p):
            for b in range(1 - q, 3 - q):
                part = dot_fine(p, q, a, b)
                total = part if total is None else total + part
        fine[2 * p + q, own(p), :] = total + fine[2 * p + q, own(p), :]
    finish(found)
    put(s_fine, pl.ds(EDGE, cols), halo(0, UP, 0, cols))
    put(s_fine, pl.ds((rows + 1) * fine_stride + EDGE, cols), halo(0, DOWN, 0, cols))
    put(s_fine, pl.ds(fine_stride + EDGE - 1, rows, stride=fine_stride), halo(0, LEFT, 0, rows))
    put(s_fine, pl.ds(fine_stride + EDGE + cols, rows, stride=fine_stride), halo(0, RIGHT, 0, rows))
    put(s_fine, pl.ds(EDGE - 1, 1), halo(0, UP_LEFT, 0, CORNER)[0:1])
    put(s_fine, pl.ds(EDGE + cols, 1), halo(0, UP_RIGHT, 0, CORNER)[0:1])
    last = (rows + 1) * fine_stride + EDGE
    put(s_fine, pl.ds(last - 1, 1), halo(0, DOWN_LEFT, 0, CORNER)[0:1])
    put(s_fine, pl.ds(last + cols, 1), halo(0, DOWN_RIGHT, 0, CORNER)[0:1])
    for i in range(rows):
        fill_feat(i, (0, 3))
    fill_feat(-1, (0, 1, 2, 3))
    fill_feat(rows, (0, 1, 2, 3))

    pooled = None
    for p, q in phases:
        total = None
        for a in range(3):
            for b in range(3):
                if p + a - 1 in (0, 1) and q + b - 1 in (0, 1):
                    continue
                part = dot_fine(p, q, a, b)
                total = part if total is None else total + part
        total = total + fine[2 * p + q, own(p), :]
        fine[2 * p + q, own(p), :] = total
        pooled = total if pooled is None else pooled + total
    pooled = (0.25 * pooled).astype(BF16).astype(F32)
    for i in range(h):
        put(s_pool, pl.ds((i + 2) * stride + EDGE, w), pooled[i * w : (i + 1) * w])

    def line(p, q, i):
        return fine[2 * p + q, (i + p) * w : (i + p + 1) * w, :]

    def column(values, j):
        put(mix, pl.ds(0, cells), values)
        return get(mix, pl.ds(j, h, stride=w))

    pool_top, pool_bottom = pooled[0 : 2 * w], pooled[(h - 2) * w :]

    def pool_column(j):
        return get(s_pool, pl.ds(2 * stride + EDGE + j, h, stride=stride))

    lefts = [column(fine[2 * p, own(p), :], 0) for p in range(2)]
    rights = [column(fine[2 * p + 1, own(p), :], w - 1) for p in range(2)]
    parts = [
        (pool_top, line(0, 0, 0), line(0, 1, 0)),
        (pool_bottom, line(1, 0, h - 1), line(1, 1, h - 1)),
        (pool_column(0), pool_column(1), *lefts),
        (pool_column(w - 2), pool_column(w - 1), *rights),
    ]
    for k in range(4):
        i, j = k // 2, k % 2
        at = (i * (h - 2) + 2) * stride + EDGE + j * (w - 2)
        cell = line(i, j, i * (h - 1))[j * (w - 1) : j * (w - 1) + 1]
        parts.append(
            corner(k, get(s_pool, pl.ds(at, 2)), get(s_pool, pl.ds(at + stride, 2)), cell)
        )
    found = start(1, (4 * w, CORNER), parts)
    for i in range(h):
        put(s_noise, pl.ds((i + 1) * stride + EDGE, w), noise_coarse[pl.ds(i * w, w), :])
    put(s_noise, pl.ds(EDGE, w), halo(0, UP, cols, w))
    put(s_noise, pl.ds((h + 1) * stride + EDGE, w), halo(0, DOWN, cols, w))
    put(s_noise, pl.ds(stride + EDGE - 1, h, stride=stride), halo(0, LEFT, rows, h))
    put(s_noise, pl.ds(stride + EDGE + w, h, stride=stride), halo(0, RIGHT, rows, h))
    put(s_noise, pl.ds(EDGE - 1, 1), halo(0, UP_LEFT, 0, CORNER)[1:2])
    put(s_noise, pl.ds(EDGE + w, 1), halo(0, UP_RIGHT, 0, CORNER)[1:2])
    last = (h + 1) * stride + EDGE
    put(s_noise, pl.ds(last - 1, 1), halo(0, DOWN_LEFT, 0, CORNER)[1:2])
    put(s_noise, pl.ds(last + w, 1), halo(0, DOWN_RIGHT, 0, CORNER)[1:2])
    finish(found)
    for k in range(2):
        put(s_pool, pl.ds(k * stride + EDGE, w), halo(1, UP, k * w, w))
        put(s_pool, pl.ds((h + 2 + k) * stride + EDGE, w), halo(1, DOWN, k * w, w))
        put(s_pool, pl.ds(2 * stride + EDGE - 2 + k, h, stride=stride), halo(1, LEFT, k * h, h))
        put(s_pool, pl.ds(2 * stride + EDGE + w + k, h, stride=stride), halo(1, RIGHT, k * h, h))
        put(s_pool, pl.ds(k * stride + EDGE - 2, 2), halo(1, UP_LEFT, 0, CORNER)[2 * k : 2 * k + 2])
        put(s_pool, pl.ds(k * stride + EDGE + w, 2), halo(1, UP_RIGHT, 0, CORNER)[2 * k : 2 * k + 2])
        at = (h + 2 + k) * stride + EDGE
        put(s_pool, pl.ds(at - 2, 2), halo(1, DOWN_LEFT, 0, CORNER)[2 * k : 2 * k + 2])
        put(s_pool, pl.ds(at + w, 2), halo(1, DOWN_RIGHT, 0, CORNER)[2 * k : 2 * k + 2])
    base = cells + w
    for q in range(2):
        fine[q, cells : cells + w, :] = halo(1, DOWN, (2 + q) * w, w)
        fine[2 + q, 0:w, :] = halo(1, UP, (2 + q) * w, w)
    for p in range(2):
        fine[2 * p, base + p : base + p + h, :] = halo(1, RIGHT, (2 + p) * h, h)
        fine[2 * p + 1, base + p : base + p + h, :] = halo(1, LEFT, (2 + p) * h, h)
    fine[3, base : base + 1, :] = halo(1, UP_LEFT, 0, CORNER)[4:5]
    fine[2, base : base + 1, :] = halo(1, UP_RIGHT, 0, CORNER)[4:5]
    fine[1, base + h : base + h + 1, :] = halo(1, DOWN_LEFT, 0, CORNER)[4:5]
    fine[0, base + h : base + h + 1, :] = halo(1, DOWN_RIGHT, 0, CORNER)[4:5]

    loads[4].wait()
    for i in range(h + 4):
        for b in range(3):
            x_pool[b, i * w : (i + 1) * w, :] = get(
                s_pool, pl.ds(i * stride + EDGE + b - 1, w)
            ).astype(BF16)
    for a in range(3):
        for b in range(3):
            both = [
                get(s_pool, pl.ds(a * stride + EDGE - 2 + b, side, stride=stride)),
                get(s_pool, pl.ds(a * stride + EDGE + w - 1 + b, side, stride=stride)),
            ]
            side_pool[3 * a + b] = jnp.concatenate(both, axis=0).astype(BF16)
    ring = (h + 2) * w
    noise = jnp.concatenate(
        [get(s_noise, pl.ds(i * stride + EDGE, w)) for i in range(h + 2)]
        + [
            get(s_noise, pl.ds(EDGE - 1, side, stride=stride)),
            get(s_noise, pl.ds(EDGE + w, side, stride=stride)),
        ],
        axis=0,
    )
    total = None
    for a in range(3):
        for b in range(3):
            x = jnp.concatenate([x_pool[b, pl.ds(a * w, ring), :], side_pool[3 * a + b]], axis=0)
            part = jnp.dot(x, tap_of(w_coarse, a, b), preferred_element_type=F32)
            total = part if total is None else total + part
    total = total + noise
    coarse[...] = total[w : w + cells]
    total = total.astype(BF16).astype(F32)
    put(s_ctx, pl.ds(EDGE, w), jnp.where(has_up, total[0:w], 0.0))
    for i in range(1, h + 1):
        put(s_ctx, pl.ds(i * stride + EDGE, w), total[i * w : (i + 1) * w])
    put(s_ctx, pl.ds((h + 1) * stride + EDGE, w), jnp.where(has_down, total[ring - w : ring], 0.0))
    place = lax.broadcasted_iota(jnp.int32, (side, chans), 0)
    first = jnp.where(has_up, 0, 1)
    limit = jnp.where(has_down, h + 2, h + 1)
    inside = jnp.logical_and(place >= first, place < limit)
    for at, has, values in (
        (EDGE - 1, has_left, total[ring : ring + side]),
        (EDGE + w, has_right, total[ring + side :]),
    ):
        put(
            s_ctx,
            pl.ds(at, side, stride=stride),
            jnp.where(jnp.logical_and(inside, has), values, 0.0),
        )
    for i in range(h + 2):
        for k in range(3):
            x_ctx[k, i * w : (i + 1) * w, :] = get(
                s_ctx, pl.ds(i * stride + EDGE + k - 1, w)
            ).astype(BF16)
    for q in range(2):
        for kr in range(2):
            for kc in range(2):
                at = kr * stride + EDGE + (w - 1 if q == 0 else -1) + kc
                side_ctx[(2 * q + kr) * 2 + kc] = get(
                    s_ctx, pl.ds(at, extra, stride=stride)
                ).astype(BF16)

    place = lax.broadcasted_iota(jnp.int32, (extra, 2 * chans), 0)
    for p, q in phases:
        prior = None
        for kr in range(2):
            for kc in range(2):
                x = jnp.concatenate(
                    [x_ctx[q + kc, pl.ds(kr * w, base), :], side_ctx[(2 * q + kr) * 2 + kc]],
                    axis=0,
                )
                part = jnp.dot(
                    x, w_sums[((2 * p + kr) * 2 + q) * 2 + kc], preferred_element_type=F32
                )
                prior = part if prior is None else prior + part
        raw = prior[:, chans:]
        small = jnp.exp(-jnp.abs(raw))
        sigma = jnp.maximum(raw, 0.0) + jnp.log1p(small) + 0.5
        whole = 1.0 + small
        both_inverse = 1.0 / (sigma * whole)
        gate = jnp.where(raw >= 0, 1.0, small) * (sigma * both_inverse)
        inverse = whole * both_inverse
        ratio = (fine[2 * p + q] - prior[:, :chans]) * inverse
        residual = ratio * inverse
        err[2 * p + q] = residual[own(p)]
        slope = (inverse - ratio * ratio * inverse) * gate
        both = jnp.concatenate([-residual, slope], axis=1).astype(BF16).astype(F32)
        if p == 0:
            g_main[q, 0:cells, :] = both[0:cells]
            g_main[q, cells:, :] = jnp.where(has_down, both[cells:base], 0.0)
            inside = jnp.logical_or(has_down, place < h)
        else:
            g_main[2 + q, 0:w, :] = jnp.where(has_up, both[0:w], 0.0)
            g_main[2 + q, w:, :] = both[w:base]
            inside = jnp.logical_or(has_up, place > 0)
        inside = jnp.logical_and(inside, has_left if q else has_right)
        g_side[2 * p + q] = jnp.where(inside, both[base:], 0.0)

    windows = ((1, 1), (0, 1), (0, 0))
    for a in range(3):
        i0, i1 = windows[a]
        for q in range(2):
            total = g_main[q, pl.ds(i0 * w, cells), :] + g_main[2 + q, pl.ds(i1 * w, cells), :]
            for i in range(h):
                put(s_pair.at[q], pl.ds(i * stride + EDGE, w), total[i * w : (i + 1) * w])
            total = g_side[q, i0 : i0 + h, :] + g_side[2 + q, i1 : i1 + h, :]
            put(s_pair.at[q], pl.ds(EDGE - 1 if q else EDGE + w, h, stride=stride), total)
        for i in range(h):
            at = i * stride + EDGE
            even, odd = get(s_pair.at[0], pl.ds(at, w)), get(s_pair.at[1], pl.ds(at, w))
            here = slice(i * w, (i + 1) * w)
            boxes[3 * a, here, :] = (odd + get(s_pair.at[0], pl.ds(at + 1, w))).astype(BF16)
            boxes[3 * a + 1, here, :] = (even + odd).astype(BF16)
            boxes[3 * a + 2, here, :] = (get(s_pair.at[1], pl.ds(at - 1, w)) + even).astype(BF16)

    total = None
    for tap in range(9):
        part = dot_out(boxes[tap], tap_of(w_prior, tap // 3, tap % 3))
        total = part if total is None else total + part
    total = (coarse[...] + total).astype(BF16).astype(F32)

    def pad_lines(values):
        for i in range(h):
            put(s_pool, pl.ds((i + 1) * stride + EDGE, w), values[i * w : (i + 1) * w])

    pad_lines(total)
    parts = [
        (total[0:w],),
        (total[cells - w :],),
        (get(s_pool, pl.ds(stride + EDGE, h, stride=stride)),),
        (get(s_pool, pl.ds(stride + EDGE + w - 1, h, stride=stride)),),
    ]
    for k in range(4):
        i, j = k // 2, k % 2
        at = (i * (h - 1) + 1) * stride + EDGE + j * (w - 1)
        parts.append(corner(k, get(s_pool, pl.ds(at, 1))))
    found = start(2, (w, CORNER), parts)
    for part in range(2):
        for tap in range(9):
            spread(
                parts_prior[2 * part : 2 * part + 2],
                tap * chans,
                dot_in(
                    x_ctx[1, pl.ds(w, cells), :], boxes[tap, :, part * chans : (part + 1) * chans]
                ),
            )
            begin(prior_chains[2 * part : 2 * part + 2], tap)
    gco = total.astype(BF16)
    for a in range(3):
        for b in range(3):
            spread(
                parts_coarse,
                (3 * a + b) * chans,
                dot_in(x_pool[b, pl.ds((a + 1) * w, cells), :], gco),
            )
            begin(middle_chains, 3 * a + b)
    advance(early)
    advance(late)
    advance(middle_chains)
    finish(found)

    put(s_pool, pl.ds(EDGE, w), halo(2, UP, 0, w))
    put(s_pool, pl.ds((h + 1) * stride + EDGE, w), halo(2, DOWN, 0, w))
    put(s_pool, pl.ds(stride + EDGE - 1, h, stride=stride), halo(2, LEFT, 0, h))
    put(s_pool, pl.ds(stride + EDGE + w, h, stride=stride), halo(2, RIGHT, 0, h))
    put(s_pool, pl.ds(EDGE - 1, 1), halo(2, UP_LEFT, 0, CORNER)[0:1])
    put(s_pool, pl.ds(EDGE + w, 1), halo(2, UP_RIGHT, 0, CORNER)[0:1])
    last = (h + 1) * stride + EDGE
    put(s_pool, pl.ds(last - 1, 1), halo(2, DOWN_LEFT, 0, CORNER)[0:1])
    put(s_pool, pl.ds(last + w, 1), halo(2, DOWN_RIGHT, 0, CORNER)[0:1])
    for i in range(h + 2):
        for k in range(3):
            x_gco[k, i * w : (i + 1) * w, :] = get(
                s_pool, pl.ds(i * stride + EDGE + k - 1, w)
            ).astype(BF16)
    total = None
    for a in range(3):
        for b in range(3):
            part = dot_out(x_gco[2 - b, pl.ds((2 - a) * w, cells), :], tap_of(w_coarse, a, b))
            total = part if total is None else total + part
    total = 0.25 * total

    for p, q in phases:
        own_gfi[2 * p + q] = (err[2 * p + q] + total).astype(BF16)

    def s_gfi(q):
        return s_pair.at[q, pl.ds(0, chans // LANES)]

    def gfi_line(p, q, i):
        return own_gfi[2 * p + q, i * w : (i + 1) * w, :]

    for p, q in phases:
        for i in range(h):
            put(
                s_gfi(q),
                pl.ds((i + p * h) * stride + EDGE, w),
                own_gfi[2 * p + q, i * w : (i + 1) * w, :].astype(F32),
            )

    def gfi_column(p, q):
        at = p * h * stride + EDGE + (w - 1 if q else 0)
        return get(s_gfi(q), pl.ds(at, h, stride=stride))

    parts = [
        (gfi_line(0, 0, 0), gfi_line(0, 1, 0)),
        (gfi_line(1, 0, h - 1), gfi_line(1, 1, h - 1)),
        (gfi_column(0, 0), gfi_column(1, 0)),
        (gfi_column(0, 1), gfi_column(1, 1)),
    ]
    for k in range(4):
        i, j = k // 2, k % 2
        at = i * (2 * h - 1) * stride + EDGE + j * (w - 1)
        parts.append(corner(k, get(s_gfi(j), pl.ds(at, 1))))
    found = start(3, (2 * w, CORNER), parts)
    for a in range(3):
        for b in range(3):
            total = None
            for p, q in phases:
                part = dot_in(view(x_feat, p + a - 1, q + b - 1), own_gfi[2 * p + q])
                total = part if total is None else total + part
            spread(parts_post, (3 * a + b) * chans, total)
            begin(post_chains, 3 * a + b)
    advance(post_chains)
    advance(prior_chains)
    advance(middle_chains)
    finish(found)
    for p in range(2):
        put(s_gfi(1), pl.ds(p * h * stride + EDGE - 1, h, stride=stride), halo(3, LEFT, p * h, h))
        put(s_gfi(0), pl.ds(p * h * stride + EDGE + w, h, stride=stride), halo(3, RIGHT, p * h, h))
        for q in range(2):
            x_gfi[p, 1 + q, p * w : p * w + cells, :] = own_gfi[2 * p + q]
            x_gfi[p, 1 + q, (1 - p) * cells : (1 - p) * cells + w, :] = halos[
                3, UP if p else DOWN, q * w : (q + 1) * w, :
            ]
        for i in range(h):
            here = slice((i + p) * w, (i + p + 1) * w)
            at = (i + p * h) * stride + EDGE
            x_gfi[p, 0, here, :] = get(s_gfi(1), pl.ds(at - 1, w)).astype(BF16)
            x_gfi[p, 3, here, :] = get(s_gfi(0), pl.ds(at + 1, w)).astype(BF16)
        ring_at = slice((1 - p) * cells, (1 - p) * cells + w)
        vertical_side = UP if p else DOWN
        left = halo(3, UP_LEFT if p else DOWN_LEFT, 0, CORNER)[0:1]
        right = halo(3, UP_RIGHT if p else DOWN_RIGHT, 0, CORNER)[0:1]
        put(s_gfi(1), pl.ds(EDGE - 1, 1), left)
        put(s_gfi(1), pl.ds(EDGE, w), halo(3, vertical_side, w, w))
        put(s_gfi(0), pl.ds(EDGE, w), halo(3, vertical_side, 0, w))
        put(s_gfi(0), pl.ds(EDGE + w, 1), right)
        x_gfi[p, 0, ring_at, :] = get(s_gfi(1), pl.ds(EDGE - 1, w)).astype(BF16)
        x_gfi[p, 3, ring_at, :] = get(s_gfi(0), pl.ds(EDGE + 1, w)).astype(BF16)
    for p, q in phases:
        total = None
        for a in range(3):
            for b in range(3):
                part = dot_out(view(x_gfi, p - a + 1, q - b + 1), tap_of(w_post, a, b))
                total = part if total is None else total + part
        for i in range(h):
            put(mix, pl.ds((2 * i + p) * cols + q, w, stride=2), total[i * w : (i + 1) * w])
    grad_feat[...] = get(mix, pl.ds(0, rows * cols)).astype(BF16)
    advance(post_chains)
    advance(prior_chains)
    advance(middle_chains)
    advance(post_chains)
    advance(prior_chains)
    advance(middle_chains)
    for _ in range(bits):
        advance(prior_chains + middle_chains + post_chains)


def hand_out(*refs):
    for source, target in zip(refs[:4], refs[4:]):
        target[...] = source[...]


def orders_of(n_row, n_col, pieces):
    bits = (n_row * n_col).bit_length() - 1
    near, a, b = (0,), 1, n_col.bit_length() - 1
    far = [k for k in range(1, bits) if k not in (a, b)]
    pairs = [tuple(far[k : k + 2]) for k in range(0, len(far), 2)]
    singles = [(k,) for k in far]
    post = (near, (a, b), *pairs)
    middle = (near, singles[0], (a, b), *singles[1:])
    prior = ((near, (b,), (a,), *pairs), (near, (a,), (b,), *pairs))
    mixed = ((post, middle)[k % 2] for k in range(pieces))
    return (*mixed, *(middle,) * pieces, *prior * pieces)


def on_device(sizes, feat, noise_fine, noise_coarse, w_post, w_coarse, w_prior):
    n_row, n_col = sizes
    rows, cols, chans = feat.shape
    h, w = rows // 2, cols // 2
    scale = 1.0 / math.sqrt(rows * n_row * cols * n_col)
    cells, quarter = rows * cols, h * w
    vmem = pl.BlockSpec(memory_space=pltpu.VMEM)
    count = n_row * n_col
    orders = orders_of(n_row, n_col, chans // LANES)
    dims = (rows, cols, chans, scale, n_row, n_col, orders)
    per = w_post.shape[0] // count
    widths = (LANES,) * len(orders)
    anywhere = pl.BlockSpec(memory_space=pl.ANY)
    extra, side, stride = round_up(h + 1, 16), round_up(h + 2, 8), w + 2 * EDGE

    def lanes(n, depth=chans):
        return pltpu.VMEM((depth // LANES, n, LANES), F32)

    grad_feat, out_post, out_coarse, out_prior = pl.pallas_call(
        functools.partial(tile_kernel, dims),
        out_shape=(
            pltpu.VMEM((cells, chans), BF16),
            pltpu.VMEM((per * chans // LANES, LANES), F32),
            pltpu.VMEM((per * chans // LANES, LANES), F32),
            pltpu.VMEM((per * 2 * chans // LANES, LANES), F32),
        ),
        in_specs=[anywhere] * 6,
        out_specs=(vmem,) * 4,
        scratch_shapes=[
            pltpu.VMEM((cells, chans), BF16),
            pltpu.VMEM((cells, chans), F32),
            pltpu.VMEM((quarter, chans), F32),
            pltpu.VMEM(w_post.shape, BF16),
            pltpu.VMEM(w_coarse.shape, BF16),
            pltpu.VMEM(w_prior.shape, BF16),
            pltpu.VMEM((4, (h + 1) * w + extra, chans), F32),
            pltpu.VMEM((4, quarter, chans), F32),
            pltpu.VMEM((quarter, chans), F32),
            lanes((rows + 2) * (cols + 2 * EDGE)),
            lanes((side + 2) * stride),
            lanes(side * stride),
            lanes((extra + 1) * stride),
            pltpu.VMEM((2, 2 * chans // LANES, max(2 * h * stride, cells), LANES), F32),
            lanes(4 * CORNER),
            pltpu.VMEM((2, 4, (h + 1) * w, chans), BF16),
            pltpu.VMEM((3, (h + 4) * w, chans), BF16),
            pltpu.VMEM((9, 2 * side, chans), BF16),
            pltpu.VMEM((3, (h + 2) * w, chans), BF16),
            pltpu.VMEM((8, extra, chans), BF16),
            pltpu.VMEM((16, chans, 2 * chans), BF16),
            pltpu.VMEM((4, (h + 1) * w, 2 * chans), F32),
            pltpu.VMEM((4, extra, 2 * chans), F32),
            pltpu.VMEM((9, quarter, 2 * chans), BF16),
            pltpu.VMEM((4, quarter, chans), BF16),
            pltpu.VMEM((4, 8, 4 * w, chans), BF16),
            pltpu.VMEM((4, 8, 4 * w, chans), BF16),
            [pltpu.VMEM((count, per, width), F32) for width in widths],
            [pltpu.VMEM((count // 2, per, width), BF16) for width in widths],
            [pltpu.VMEM((count - 1, per, width), BF16) for width in widths],
            pltpu.SemaphoreType.DMA((4, 16)),
            pltpu.SemaphoreType.DMA((len(orders), max(map(len, orders)), 3, 2)),
            pltpu.SemaphoreType.DMA((6,)),
        ],
        compiler_params=pltpu.CompilerParams(
            collective_id=0, has_side_effects=True, vmem_limit_bytes=62 * 2**20
        ),
    )(
        feat.reshape(cells, chans),
        noise_fine.reshape(cells, chans),
        noise_coarse.reshape(quarter, chans),
        w_post,
        w_coarse,
        w_prior,
    )
    results = tuple(
        pltpu.with_memory_space_constraint(a, pltpu.VMEM)
        for a in (grad_feat, out_post, out_coarse, out_prior)
    )
    grad_feat, out_post, out_coarse, out_prior = pl.pallas_call(
        hand_out,
        out_shape=tuple(jax.ShapeDtypeStruct(a.shape, a.dtype) for a in results),
        in_specs=[vmem] * 4,
        out_specs=(vmem,) * 4,
    )(*results)
    return (
        grad_feat.reshape(rows, cols, chans),
        out_post.reshape(-1),
        out_coarse.reshape(-1),
        out_prior.reshape(-1),
    )


def solution(mesh):
    sizes = (mesh.shape["row"], mesh.shape["col"])
    return jax.shard_map(
        functools.partial(on_device, sizes),
        mesh=mesh,
        in_specs=(
            P("row", "col", None),
            P("row", "col", None),
            P("row", "col", None),
            P(),
            P(),
            P(),
        ),
        out_specs=(P("row", "col", None), P(("row", "col")), P(("row", "col")), P(("row", "col"))),
        check_vma=False,
    )
```
